32 devices in a mesh: node: 8 (over z, x), feat: 4 (over y, core).
Axes of the slice: x: 2, y: 2, z: 4, core: 2. Of those that a mesh axis runs over, the one named last changes fastest.
Arguments:
- feature_table: bfloat16 [8192, 2048], P('node', 'feat'), may hold values from -6 to 6
- hub_table: bfloat16 [32, 2048], P('node', 'feat'), may hold values from -6 to 6
- first_self: bfloat16 [2048, 2048], P('feat'), may hold values from -0.125 to 0.125
- first_pooled: bfloat16 [2048, 2048], P('feat'), may hold values from -0.125 to 0.125
- second_self: bfloat16 [2048, 256], P('feat'), may hold values from -0.125 to 0.125
- second_pooled: bfloat16 [2048, 256], P('feat'), may hold values from -0.125 to 0.125
- first_lists: int32 [3072, 10], P('node'), may hold values from 0 to 8223, as said below
- first_counts: int32 [3072], P('node'), may hold values from 1 to 10
- second_lists: int32 [2048, 5], P('node'), may hold values from 0 to 3071, as said below
- second_counts: int32 [2048], P('node'), may hold values from 1 to 5
Outputs:
- embedding: bfloat16 [2048, 256], P(('node', 'feat'))
The draws below stay inside these ranges and needn't reach their ends.
Inputs may be any that keep to these rules, and one draw needn't show every extreme that they name: `first_lists`: an entry below 8192 names a row of feature_table, held by node shard (entry // 1024); an entry v of 8192 or more names hub clip v - 8192, owned by node shard (v - 8192) // 4. Slots at or beyond a clip's count are padding and still hold such entries. Of the 3840 entries of one node shard's rows, padding included, at most 480 name feature rows held by any one node shard; in every draw one node shard is named exactly 480 times by the rows of every node shard. `second_lists`: entries name frontier clips, held by node shard (entry // 384). Of the 1280 entries of one node shard's rows, padding included, exactly 160 name frontier clips of each node shard.
All inputs are finite; a program needn't handle non-finite values.
Results may differ from the reference program's by a relative error of at most 0.0052.
Values may be sent and summed in bfloat16 or wider, within the bound.
A program may use at most 64 MiB of HBM per device.

```python
import jax
import jax.numpy as jnp
from jax import lax

F = 2048
H = 2048
O = 256
FAN1 = 10
FAN2 = 5
ROWS_DEV = 1024
FRONT_DEV = 384
TGT_DEV = 256
NROWS = 8192
HUBS = 32
FRONT = 3072
TARGETS = 2048
CAP1 = 480
CAP2 = 160
N_NODE = 8
N_FEAT = 4


def draw_first_lists(key, part):
    shards = NROWS // ROWS_DEV
    slots = FRONT_DEV * FAN1
    keys = jax.random.split(jax.random.fold_in(key, 11), 7)
    levels = jax.random.randint(keys[0], (shards, shards), 1, 9)
    favoured = jax.random.randint(keys[1], (), 0, shards)
    columns = jnp.arange(shards, dtype=jnp.int32)[None, :]
    levels = jnp.where(columns == favoured, 8, levels)
    second_full = jax.random.randint(keys[2], (shards, 1), 0, shards)
    levels = jnp.where(columns == second_full, 8, levels)
    owner = jnp.arange(slots, dtype=jnp.int32) // CAP1
    coin = jax.random.randint(keys[3], (shards, slots), 0, 8)
    live = coin < jnp.take(levels, owner, axis=1)
    drawn = jax.random.randint(keys[4], (shards, slots), 0, ROWS_DEV) + owner[None, :] * ROWS_DEV
    hubward = NROWS + jax.random.randint(keys[5], (shards, slots), 0, HUBS)
    entries = jnp.where(live, drawn, hubward)
    rows_index = jnp.arange(shards, dtype=jnp.int32)[:, None]
    slot_index = jnp.arange(slots, dtype=jnp.int32)[None, :]
    entries = jnp.where((rows_index == 0) & (slot_index == 0), 0, entries)
    other_owner = (favoured + 1) % shards
    top_slot = other_owner * CAP1 + CAP1 - 1
    entries = jnp.where((rows_index == 0) & (slot_index == top_slot), NROWS + HUBS - 1, entries)
    shuffle_keys = jax.random.split(keys[6], shards)
    order = jax.vmap(lambda one_key: jax.random.permutation(one_key, slots))(shuffle_keys)
    entries = jnp.take_along_axis(entries, order, axis=1)
    return entries.reshape(shards * FRONT_DEV, FAN1).astype(jnp.int32)


def draw_second_lists(key, part):
    shards = NROWS // ROWS_DEV
    slots = TGT_DEV * FAN2
    choose_key, shuffle_key = jax.random.split(jax.random.fold_in(key, 31))
    owner = jnp.arange(slots, dtype=jnp.int32) // CAP2
    picks = jax.random.randint(choose_key, (shards, slots), 0, FRONT_DEV) + owner[None, :] * FRONT_DEV
    rows_index = jnp.arange(shards, dtype=jnp.int32)[:, None]
    slot_index = jnp.arange(slots, dtype=jnp.int32)[None, :]
    picks = jnp.where((rows_index == 0) & (slot_index == 0), 0, picks)
    picks = jnp.where((rows_index == 0) & (slot_index == slots - 1), shards * FRONT_DEV - 1, picks)
    shuffle_keys = jax.random.split(shuffle_key, shards)
    order = jax.vmap(lambda one_key: jax.random.permutation(one_key, slots))(shuffle_keys)
    picks = jnp.take_along_axis(picks, order, axis=1)
    return picks.reshape(shards * TGT_DEV, FAN2).astype(jnp.int32)


def count_draw(key, salt, total, fanout):
    coin_key, value_key = jax.random.split(jax.random.fold_in(key, salt))
    values = jax.random.randint(value_key, (total,), 1, fanout + 1)
    coin = jax.random.randint(coin_key, (total,), 0, 5)
    counts = jnp.where(coin < 3, fanout, values)
    position = jnp.arange(total, dtype=jnp.int32)
    counts = jnp.where(position == 0, fanout, counts)
    counts = jnp.where(position == 1, 1, counts)
    return counts.astype(jnp.int32)


def draw_first_counts(key, part):
    return count_draw(key, 41, NROWS // ROWS_DEV * FRONT_DEV, FAN1)


def draw_second_counts(key, part):
    return count_draw(key, 43, NROWS // ROWS_DEV * TGT_DEV, FAN2)


def block_scale(own_key, shape, cuts, low, top_value):
    level = 1.0
    for axis_at, blocks in cuts:
        heights = jax.random.uniform(jax.random.fold_in(jax.random.fold_in(own_key, 6), axis_at), (blocks,), jnp.float32, low / len(cuts), top_value / len(cuts))
        level = level * jnp.repeat(jnp.exp(heights), shape[axis_at] // blocks).reshape((-1,) + (1,) * (len(shape) - 1 - axis_at))
    return level


def gaussian(rng, shape, scale, most, pieces=(), kind=jnp.bfloat16):
    drawn = jax.random.normal(rng, shape, jnp.float32) * scale
    if len(pieces) > 0:
        drawn = block_scale(rng, shape, pieces, -0.22, 0.18) * drawn
    return jnp.clip(drawn, min=-most, max=most).astype(kind)


def setup_inputs(seed: int = 0) -> dict:
    streams_of = jax.random.split(jax.random.key(seed), 11)
    feature_table = gaussian(streams_of[0], (NROWS, F), 1.0, 6.0, ((0, 8), (1, 4)))
    hub_table = gaussian(streams_of[1], (HUBS, F), 1.0, 6.0, ((0, 8), (1, 4)))
    first_self = gaussian(streams_of[2], (F, H), F ** -0.5, 0.125, ((0, 4),))
    first_pooled = gaussian(streams_of[3], (F, H), F ** -0.5, 0.125, ((0, 4),))
    second_self = gaussian(streams_of[4], (H, O), H ** -0.5, 0.125, ((0, 4),))
    second_pooled = gaussian(streams_of[5], (H, O), H ** -0.5, 0.125, ((0, 4),))
    first_lists = draw_first_lists(jax.random.fold_in(streams_of[10], 71), 0)
    first_counts = draw_first_counts(jax.random.fold_in(streams_of[10], 71), 0)
    second_lists = draw_second_lists(jax.random.fold_in(streams_of[10], 71), 0)
    second_counts = draw_second_counts(jax.random.fold_in(streams_of[10], 71), 0)
    return dict(feature_table=feature_table, hub_table=hub_table, first_self=first_self, first_pooled=first_pooled, second_self=second_self, second_pooled=second_pooled, first_lists=first_lists, first_counts=first_counts, second_lists=second_lists, second_counts=second_counts)


def first_block(shard, pooled, feature_table, self_split, pool_split, first_lists, first_counts):
    begin = (shard * FRONT_DEV).astype(jnp.int32)
    lists = lax.dynamic_slice_in_dim(first_lists, begin, FRONT_DEV, 0)
    counts = lax.dynamic_slice_in_dim(first_counts, begin, FRONT_DEV, 0)
    picked = jnp.take(pooled, lists, axis=0).astype(jnp.float32)
    valid = jnp.arange(FAN1, dtype=jnp.int32)[None, :] < counts[:, None]
    summed = lax.optimization_barrier(jnp.sum(jnp.where(valid[:, :, None], picked, jnp.float32(0.0)), axis=1))
    first_mean = (summed / counts[:, None].astype(jnp.float32)).astype(jnp.bfloat16)
    own_rows = lax.dynamic_slice_in_dim(feature_table, (shard * ROWS_DEV).astype(jnp.int32), FRONT_DEV, 0)
    group = F // N_FEAT
    own_split = own_rows.astype(jnp.float32).reshape(FRONT_DEV, N_FEAT, group)
    mean_split = first_mean.astype(jnp.float32).reshape(FRONT_DEV, N_FEAT, group)
    parts = jnp.einsum('rgc,gch->grh', own_split, self_split, precision=lax.Precision.HIGHEST)
    parts = parts + jnp.einsum('rgc,gch->grh', mean_split, pool_split, precision=lax.Precision.HIGHEST)
    return jax.nn.relu(lax.optimization_barrier(jnp.sum(parts, axis=0))).astype(jnp.bfloat16)

def second_block(shard, hidden, second_self, second_pooled, second_lists, second_counts):
    begin = (shard * TGT_DEV).astype(jnp.int32)
    lists = lax.dynamic_slice_in_dim(second_lists, begin, TGT_DEV, 0)
    counts = lax.dynamic_slice_in_dim(second_counts, begin, TGT_DEV, 0)
    picked = jnp.take(hidden, lists, axis=0).astype(jnp.float32)
    valid = jnp.arange(FAN2, dtype=jnp.int32)[None, :] < counts[:, None]
    summed = lax.optimization_barrier(jnp.sum(jnp.where(valid[:, :, None], picked, jnp.float32(0.0)), axis=1))
    second_mean = (summed / counts[:, None].astype(jnp.float32)).astype(jnp.bfloat16)
    own_hidden = lax.dynamic_slice_in_dim(hidden, (shard * FRONT_DEV).astype(jnp.int32), TGT_DEV, 0)
    mixed = jnp.dot(own_hidden, second_self, preferred_element_type=jnp.float32)
    mixed = mixed + jnp.dot(second_mean, second_pooled, preferred_element_type=jnp.float32)
    scale = lax.rsqrt(lax.optimization_barrier(jnp.mean(mixed * mixed, axis=1, keepdims=True)) + 1e-06)
    return (mixed * scale).astype(jnp.bfloat16)

def reference(feature_table, hub_table, first_self, first_pooled, second_self, second_pooled, first_lists, first_counts, second_lists, second_counts):
    pooled = jnp.concatenate([feature_table, hub_table], axis=0)
    group = F // N_FEAT
    self_split = first_self.astype(jnp.float32).reshape(N_FEAT, group, H)
    pool_split = first_pooled.astype(jnp.float32).reshape(N_FEAT, group, H)
    shards = jnp.arange(N_NODE, dtype=jnp.int32)
    hidden = lax.map(lambda shard: first_block(shard, pooled, feature_table, self_split, pool_split, first_lists, first_counts), shards)
    hidden = hidden.reshape(FRONT, H)
    embedding = lax.map(lambda shard: second_block(shard, hidden, second_self, second_pooled, second_lists, second_counts), shards)
    return embedding.reshape(TARGETS, O)
```

```python
import jax
import jax.numpy as jnp
from jax import lax
from jax.sharding import PartitionSpec as P


def count_matrix(local, width):
    columns = jnp.arange(width, dtype=jnp.int32)[None, :]
    total = jnp.zeros((local.shape[0], width), jnp.float32)
    for k in range(local.shape[1]):
        total = total + (local[:, k : k + 1] == columns).astype(jnp.float32)
    return total.astype(jnp.bfloat16)


def body(
    feature_table,
    hub_table,
    first_self,
    first_pooled,
    second_self,
    second_pooled,
    first_lists,
    first_counts,
    second_lists,
    second_counts,
):
    shards = lax.axis_size("node")
    me = lax.axis_index("node")
    rows_here = feature_table.shape[0]
    hubs_here = hub_table.shape[0]
    front_here, fan_one = first_lists.shape
    targets_here, fan_two = second_lists.shape
    total_rows = rows_here * shards

    slots_one = jnp.arange(fan_one, dtype=jnp.int32)[None, :]
    slots_two = jnp.arange(fan_two, dtype=jnp.int32)[None, :]
    lists_one = jnp.where(slots_one < first_counts[:, None], first_lists, -1)
    lists_two = jnp.where(slots_two < second_counts[:, None], second_lists, -1)
    packed = jnp.concatenate(
        [lists_one.reshape(-1), lists_two.reshape(-1), second_counts]
    ).reshape(1, -1)
    everyone = lax.all_gather(packed, "node", axis=0, tiled=True)
    cut_one = front_here * fan_one
    cut_two = cut_one + targets_here * fan_two
    all_one = everyone[:, :cut_one].reshape(shards * front_here, fan_one)
    all_two = everyone[:, cut_one:cut_two].reshape(shards * targets_here, fan_two)
    all_counts = everyone[:, cut_two:].reshape(shards * targets_here, 1)

    feature_at = all_one - me * rows_here
    hub_at = all_one - total_rows - me * hubs_here
    local_one = jnp.where(
        (feature_at >= 0) & (feature_at < rows_here) & (all_one >= 0),
        feature_at,
        jnp.where((hub_at >= 0) & (hub_at < hubs_here), hub_at + rows_here, -1),
    )
    combined = jnp.concatenate([feature_table, hub_table], axis=0)
    matrix_one = count_matrix(local_one, rows_here + hubs_here)
    sums = jnp.dot(matrix_one, combined, preferred_element_type=jnp.float32)
    sums = lax.psum_scatter(sums.astype(jnp.bfloat16), "node", scatter_dimension=0, tiled=True)
    first_mean = (
        sums.astype(jnp.float32) / first_counts[:, None].astype(jnp.float32)
    ).astype(jnp.bfloat16)

    part = jnp.dot(feature_table[:front_here], first_self, preferred_element_type=jnp.float32)
    part = part + jnp.dot(first_mean, first_pooled, preferred_element_type=jnp.float32)
    hidden = jax.nn.relu(
        lax.psum_scatter(part.astype(jnp.bfloat16), "feat", scatter_dimension=1, tiled=True)
    )

    projected = jnp.dot(hidden, second_pooled, preferred_element_type=jnp.float32)
    own = jnp.dot(hidden[:targets_here], second_self, preferred_element_type=jnp.float32)
    local_two = jnp.where(all_two >= 0, all_two - me * front_here, -1)
    matrix_two = count_matrix(local_two, front_here)
    mixed = jnp.dot(
        matrix_two, projected.astype(jnp.bfloat16), preferred_element_type=jnp.float32
    ) / all_counts.astype(jnp.float32)
    here = lax.dynamic_slice_in_dim(mixed, me * targets_here, targets_here, 0)
    mixed = lax.dynamic_update_slice_in_dim(mixed, here + own, me * targets_here, 0)
    mixed = lax.psum_scatter(mixed, ("node", "feat"), scatter_dimension=0, tiled=True)
    scale = lax.rsqrt(jnp.mean(mixed * mixed, axis=1, keepdims=True) + 1e-06)
    return (mixed * scale).astype(jnp.bfloat16)


def solution(mesh):
    return jax.shard_map(
        body,
        mesh=mesh,
        in_specs=(
            P("node", "feat"),
            P("node", "feat"),
            P("feat", None),
            P("feat", None),
            P("feat", None),
            P("feat", None),
            P("node", None),
            P("node"),
            P("node", None),
            P("node"),
        ),
        out_specs=P(("node", "feat"), None),
        check_vma=False,
    )
```

```python
import functools

import jax
import jax.numpy as jnp
from jax import lax
from jax.experimental import pallas as pl
from jax.experimental.pallas import tpu as pltpu
from jax.sharding import PartitionSpec as P

MESH = pl.DeviceIdType.MESH
CORES = 2


def greet(peers):
    barrier = pltpu.get_barrier_semaphore()
    for peer in peers:
        pl.semaphore_signal(barrier, inc=1, device_id=peer, device_id_type=MESH)
    pl.semaphore_wait(barrier, len(peers))


def remote(src, dst, sends, recvs, peer):
    return pltpu.make_async_remote_copy(
        src_ref=src, dst_ref=dst, send_sem=sends, recv_sem=recvs, device_id=peer, device_id_type=MESH
    )


def gather_kernel(shards, own_ref, all_ref, sends, recvs, here):
    me = lax.axis_index("node")
    peers = [{"node": lax.rem(me + off, shards)} for off in range(1, shards)]
    greet(peers)
    copies = []
    for at, peer in enumerate(peers):
        copy = remote(own_ref, all_ref.at[me], sends.at[at], recvs.at[at], peer)
        copy.start()
        copies.append(copy)
    local = pltpu.make_async_copy(own_ref, all_ref.at[me], here)
    local.start()
    local.wait()
    for copy in copies:
        copy.wait()


def gather_lists(packed, shards):
    return pl.pallas_call(
        functools.partial(gather_kernel, shards),
        out_shape=jax.ShapeDtypeStruct((shards,) + packed.shape, packed.dtype),
        in_specs=[pl.BlockSpec(memory_space=pltpu.VMEM)],
        out_specs=pl.BlockSpec(memory_space=pltpu.VMEM),
        scratch_shapes=[
            pltpu.SemaphoreType.DMA((shards - 1,)),
            pltpu.SemaphoreType.DMA((shards - 1,)),
            pltpu.SemaphoreType.DMA,
        ],
        compiler_params=pltpu.CompilerParams(collective_id=0, has_side_effects=True),
    )(packed)


def count_tiles(local, fan, width, out_ref, row0):
    rows = local.shape[0]
    for start in range(0, width, 128):
        columns = lax.broadcasted_iota(jnp.int32, (rows, 128), 1) + start
        total = jnp.zeros((rows, 128), jnp.float32)
        for k in range(fan):
            total = total + jnp.where(local[:, k : k + 1] == columns, 1.0, 0.0)
        out_ref[pl.ds(row0, rows), start : start + 128] = total.astype(jnp.bfloat16)


def main_kernel(
    sizes,
    table_ref,
    hub_ref,
    self_one,
    pool_one,
    self_two,
    pool_two,
    local_one,
    local_two,
    counts_ref,
    out_ref,
    matrix,
    matrix_two,
    hubs,
    acc,
    x_send,
    x_recv,
    z_send,
    z_recv,
    part,
    c_send,
    c_recv,
    y_send,
    y_recv,
    mixed,
    mc_recv,
    my_send,
    my_recv,
    mx_send,
    mx_recv,
    mz_send,
    mz_recv,
    x_ss,
    x_rs,
    z_ss,
    z_rs,
    c_ss,
    c_rs,
    y_ss,
    y_rs,
    mc_ss,
    mc_rs,
    my_ss,
    my_rs,
    mx_ss,
    mx_rs,
    mz_ss,
    mz_rs,
):
    big_z, big_x, big_y, fan_one, fan_two = sizes
    f32, bf16 = jnp.float32, jnp.bfloat16
    node = lax.axis_index("node")
    feat = lax.axis_index("feat")
    z, x = node // big_x, lax.rem(node, big_x)
    y, core = feat // CORES, lax.rem(feat, CORES)
    x_peers = [{"node": z * big_x + lax.rem(x + o, big_x)} for o in range(1, big_x)]
    z_peers = [{"node": lax.rem(z + o, big_z) * big_x + x} for o in range(1, big_z)]
    y_peers = [{"feat": lax.rem(y + o, big_y) * CORES + core} for o in range(1, big_y)]
    other = 1 - core
    c_peer = {"feat": y * CORES + other}
    greet(x_peers + z_peers + y_peers + [c_peer])

    rows, width = table_ref.shape
    front = acc.shape[0]
    reach = matrix.shape[1]
    hubs[...] = jnp.zeros_like(hubs)
    hubs[0 : hub_ref.shape[0], :] = hub_ref[...]

    def sums_for(target):
        def fill(at, carry):
            row0 = pl.multiple_of(at * 32, 32)
            local = local_one[pl.ds(pl.multiple_of(target * front + row0, 32), 32), :]
            count_tiles(local, fan_one, reach, matrix, row0)
            return carry

        lax.fori_loop(0, front // 32, fill, 0)
        return jnp.dot(
            matrix[:, 0:rows], table_ref[...], preferred_element_type=f32
        ) + jnp.dot(matrix[:, rows:reach], hubs[...], preferred_element_type=f32)

    def x_copy(s, o):
        return remote(
            x_send.at[s, o], x_recv.at[s, o], x_ss.at[s, o], x_rs.at[s, o], x_peers[o]
        )

    def first_phase(s, carry):
        zt = lax.rem(z + 1 + s, big_z)
        for o in range(big_x - 1):
            x_send[s, o] = sums_for(zt * big_x + lax.rem(x + 1 + o, big_x)).astype(bf16)
            x_copy(s, o).start()
        return carry

    lax.fori_loop(0, big_z, first_phase, 0)

    def z_copy(s, to):
        peer = {"node": to * big_x + x}
        return remote(z_send.at[s], z_recv.at[s], z_ss.at[s], z_rs.at[s], peer)

    def second_phase(s, carry):
        zt = lax.rem(z + 1 + s, big_z)
        acc[...] = sums_for(zt * big_x + x)
        for o in range(big_x - 1):
            x_copy(s, o).wait()
            acc[...] += x_recv[s, o].astype(f32)

        @pl.when(s < big_z - 1)
        def _():
            z_send[s] = acc[...].astype(bf16)
            z_copy(s, zt).start()

        return carry

    lax.fori_loop(0, big_z, second_phase, 0)

    hidden_part = part.shape[2]
    feats = big_y * CORES

    def own_part(f, carry):
        at = pl.ds(pl.multiple_of(f * hidden_part, 128), hidden_part)
        part[f] = jnp.dot(table_ref[0:front, :], self_one[:, at], preferred_element_type=f32)
        return carry

    lax.fori_loop(0, feats, own_part, 0)
    targets = matrix_two.shape[0]

    def fill_two(at, carry):
        row0 = pl.multiple_of(at * 32, 32)
        count_tiles(local_two[pl.ds(row0, 32), :], fan_two, front, matrix_two, row0)
        return carry

    lax.fori_loop(0, targets // 32, fill_two, 0)

    for s in range(big_z - 1):
        z_copy(s, lax.rem(z + 1 + s, big_z)).wait()
        acc[...] += z_recv[s].astype(f32)
    mean = (acc[...] / counts_ref[...].astype(f32)).astype(bf16)
    matrix[:, 0:width] = mean

    def part_of(f):
        at = pl.ds(pl.multiple_of(f * hidden_part, 128), hidden_part)
        return part[f] + jnp.dot(matrix[:, 0:width], pool_one[:, at], preferred_element_type=f32)

    def c_copy(s):
        return remote(c_send.at[s], c_recv.at[s], c_ss.at[s], c_rs.at[s], c_peer)

    def c_phase(s, carry):
        yt = lax.rem(y + 1 + s, big_y)
        c_send[s] = part_of(yt * CORES + other)
        c_copy(s).start()
        return carry

    lax.fori_loop(0, big_y, c_phase, 0)

    def y_copy(s, to):
        peer = {"feat": to * CORES + core}
        return remote(y_send.at[s], y_recv.at[s], y_ss.at[s], y_rs.at[s], peer)

    def y_step(s, carry):
        yt = lax.rem(y + 1 + s, big_y)
        total = part_of(yt * CORES + core)
        c_copy(s).wait()
        total = total + c_recv[s]

        @pl.when(s < big_y - 1)
        def _():
            y_send[s] = total.astype(bf16)
            y_copy(s, yt).start()

        @pl.when(s == big_y - 1)
        def _():
            c_send[s] = total

        return carry

    lax.fori_loop(0, big_y, y_step, 0)
    total = c_send[big_y - 1]
    for s in range(big_y - 1):
        y_copy(s, lax.rem(y + 1 + s, big_y)).wait()
        total = total + y_recv[s].astype(f32)
    hidden = jnp.maximum(total, 0.0).astype(bf16)

    projected = jnp.dot(hidden, pool_two[...], preferred_element_type=f32).astype(bf16)
    piece = out_ref.shape[0]
    own = jnp.dot(hidden[0 : piece * feats], self_two[...], preferred_element_type=f32)
    quarter = big_x * big_z * piece
    for c in range(CORES):
        for yy in range(big_y):
            at = (c * big_y + yy) * quarter
            weight = 1.0 / local_two[at : at + quarter, fan_two : fan_two + 1].astype(f32)
            mixed[c, yy] = (
                jnp.dot(matrix_two[at : at + quarter, :], projected, preferred_element_type=f32)
                * weight
            )
            row = pl.multiple_of((x * big_z + z) * piece, 8)
            f = yy * CORES + c
            mixed[c, yy, pl.ds(row, piece), :] += own[f * piece : (f + 1) * piece]

    mc = remote(mixed.at[other], mc_recv, mc_ss, mc_rs, c_peer)
    mc.start()
    mc.wait()
    y_copies = []
    for o in range(big_y - 1):
        yt = lax.rem(y + 1 + o, big_y)
        my_send[o] = (mixed[core, yt] + mc_recv[yt]).astype(bf16)
        copy = remote(my_send.at[o], my_recv.at[o], my_ss.at[o], my_rs.at[o], y_peers[o])
        copy.start()
        y_copies.append(copy)
    total = mixed[core, y] + mc_recv[y]
    for o, copy in enumerate(y_copies):
        copy.wait()
        total = total + my_recv[o].astype(f32)
    mixed[core, y] = total
    slab = big_z * piece
    x_copies = []
    for o in range(big_x - 1):
        row = pl.multiple_of(lax.rem(x + 1 + o, big_x) * slab, 8)
        mx_send[o] = mixed[core, y, pl.ds(row, slab), :].astype(bf16)
        copy = remote(mx_send.at[o], mx_recv.at[o], mx_ss.at[o], mx_rs.at[o], x_peers[o])
        copy.start()
        x_copies.append(copy)
    total = mixed[core, y, pl.ds(pl.multiple_of(x * slab, 8), slab), :]
    for o, copy in enumerate(x_copies):
        copy.wait()
        total = total + mx_recv[o].astype(f32)
    mz_send[...] = total
    z_copies = []
    for o in range(big_z - 1):
        row = pl.multiple_of(lax.rem(z + 1 + o, big_z) * piece, 8)
        copy = remote(
            mz_send.at[pl.ds(row, piece)], mz_recv.at[o], mz_ss.at[o], mz_rs.at[o], z_peers[o]
        )
        copy.start()
        z_copies.append(copy)
    total = mz_send[pl.ds(pl.multiple_of(z * piece, 8), piece), :]
    for o, copy in enumerate(z_copies):
        copy.wait()
        total = total + mz_recv[o]
    scale = lax.rsqrt(jnp.mean(total * total, axis=1, keepdims=True) + 1e-06)
    out_ref[...] = (total * scale).astype(bf16)


def body(
    feature_table,
    hub_table,
    first_self,
    first_pooled,
    second_self,
    second_pooled,
    first_lists,
    first_counts,
    second_lists,
    second_counts,
):
    shards = lax.axis_size("node")
    feats = lax.axis_size("feat")
    big_x = 2 ** ((shards.bit_length() - 1) // 2)
    big_z = shards // big_x
    big_y = feats // CORES
    me = lax.axis_index("node")
    rows_here, width = feature_table.shape
    hubs_here = hub_table.shape[0]
    front, fan_one = first_lists.shape
    targets_here, fan_two = second_lists.shape
    total_rows = rows_here * shards
    piece = targets_here // feats
    out_width = second_self.shape[1]
    hidden_part = second_self.shape[0]

    slots_one = jnp.arange(fan_one, dtype=jnp.int32)[None, :]
    slots_two = jnp.arange(fan_two, dtype=jnp.int32)[None, :]
    lists_one = jnp.where(slots_one < first_counts[:, None], first_lists, -1).T
    lists_two = jnp.where(slots_two < second_counts[:, None], second_lists, -1).T
    lists_two = jnp.concatenate([lists_two, second_counts[None, :]], axis=0)
    lists_two = jnp.pad(lists_two, ((0, 0), (0, front - targets_here)))
    packed = jnp.concatenate([lists_one, lists_two], axis=0)
    everyone = gather_lists(packed, shards)
    all_one = everyone[:, :fan_one].transpose(0, 2, 1).reshape(shards * front, fan_one)
    all_two = everyone[:, fan_one:, :targets_here]

    feature_at = all_one - me * rows_here
    hub_at = all_one - total_rows - me * hubs_here
    local_one = jnp.where(
        (feature_at >= 0) & (feature_at < rows_here) & (all_one >= 0),
        feature_at,
        jnp.where((hub_at >= 0) & (hub_at < hubs_here), hub_at + rows_here, -1),
    )
    is_count = (jnp.arange(fan_two + 1) == fan_two)[None, :, None]
    local_two = jnp.where(
        is_count, all_two, jnp.where(all_two >= 0, all_two - me * front, -1)
    )
    local_two = local_two.reshape(big_z, big_x, fan_two + 1, big_y, CORES, piece)
    local_two = local_two.transpose(4, 3, 1, 0, 5, 2).reshape(-1, fan_two + 1)

    reach = rows_here + 128
    bf16, f32 = jnp.bfloat16, jnp.float32
    dma = pltpu.SemaphoreType.DMA
    zs, xs, ys = big_z - 1, big_x - 1, big_y - 1
    quarter = big_x * big_z * piece
    slab = big_z * piece
    block = (front, width)
    hblock = (front, hidden_part)
    vmem = pl.BlockSpec(memory_space=pltpu.VMEM)
    return pl.pallas_call(
        functools.partial(main_kernel, (big_z, big_x, big_y, fan_one, fan_two)),
        out_shape=jax.ShapeDtypeStruct((piece, out_width), bf16),
        in_specs=[vmem] * 9,
        out_specs=vmem,
        scratch_shapes=[
            pltpu.VMEM((front, reach), bf16),
            pltpu.VMEM((targets_here * shards, front), bf16),
            pltpu.VMEM((128, width), bf16),
            pltpu.VMEM(block, f32),
            pltpu.VMEM((big_z, xs) + block, bf16),
            pltpu.VMEM((big_z, xs) + block, bf16),
            pltpu.VMEM((zs,) + block, bf16),
            pltpu.VMEM((zs,) + block, bf16),
            pltpu.VMEM((feats,) + hblock, f32),
            pltpu.VMEM((big_y,) + hblock, f32),
            pltpu.VMEM((big_y,) + hblock, f32),
            pltpu.VMEM((ys,) + hblock, bf16),
            pltpu.VMEM((ys,) + hblock, bf16),
            pltpu.VMEM((CORES, big_y, quarter, out_width), f32),
            pltpu.VMEM((big_y, quarter, out_width), f32),
            pltpu.VMEM((ys, quarter, out_width), bf16),
            pltpu.VMEM((ys, quarter, out_width), bf16),
            pltpu.VMEM((xs, slab, out_width), bf16),
            pltpu.VMEM((xs, slab, out_width), bf16),
            pltpu.VMEM((slab, out_width), f32),
            pltpu.VMEM((zs, piece, out_width), f32),
            dma((big_z, xs)),
            dma((big_z, xs)),
            dma((zs,)),
            dma((zs,)),
            dma((big_y,)),
            dma((big_y,)),
            dma((ys,)),
            dma((ys,)),
            dma,
            dma,
            dma((ys,)),
            dma((ys,)),
            dma((xs,)),
            dma((xs,)),
            dma((zs,)),
            dma((zs,)),
        ],
        compiler_params=pltpu.CompilerParams(
            collective_id=1, has_side_effects=True, vmem_limit_bytes=60 * 1024 * 1024
        ),
    )(
        feature_table,
        hub_table,
        first_self,
        first_pooled,
        second_self,
        second_pooled,
        local_one,
        local_two,
        first_counts[:, None],
    )


def solution(mesh):
    return jax.shard_map(
        body,
        mesh=mesh,
        in_specs=(
            P("node", "feat"),
            P("node", "feat"),
            P("feat", None),
            P("feat", None),
            P("feat", None),
            P("feat", None),
            P("node", None),
            P("node"),
            P("node", None),
            P("node"),
        ),
        out_specs=P(("node", "feat"), None),
        check_vma=False,
    )
```

```python
import functools

import jax
import jax.numpy as jnp
from jax import lax
from jax.experimental import pallas as pl
from jax.experimental.pallas import tpu as pltpu
from jax.sharding import PartitionSpec as P

MESH = pl.DeviceIdType.MESH
CORES = 2


def greet(peers):
    barrier = pltpu.get_barrier_semaphore()
    for peer in peers:
        pl.semaphore_signal(barrier, inc=1, device_id=peer, device_id_type=MESH)
    pl.semaphore_wait(barrier, len(peers))


def remote(src, dst, sends, recvs, peer):
    return pltpu.make_async_remote_copy(
        src_ref=src, dst_ref=dst, send_sem=sends, recv_sem=recvs, device_id=peer, device_id_type=MESH
    )


def count_tiles(local, fan, width, store):
    rows = local.shape[0]
    local = local.astype(jnp.int16)
    one, zero = jnp.bfloat16(1), jnp.bfloat16(0)
    for start in range(0, width, 128):
        columns = (lax.broadcasted_iota(jnp.int32, (rows, 128), 1) + start).astype(jnp.int16)
        total = jnp.zeros((rows, 128), jnp.bfloat16)
        for k in range(fan):
            picked = jnp.broadcast_to(local[:, k : k + 1], (rows, 128))
            total = total + jnp.where(picked == columns, one, zero)
        store(start, total)


def main_kernel(
    sizes,
    table_ref,
    hub_ref,
    self_one,
    pool_one,
    self_two,
    pool_two,
    packed_ref,
    counts_ref,
    out_ref,
    lists,
    local,
    tables,
    matrix,
    matrix_two,
    weights,
    means,
    acc,
    z_send,
    z_recv,
    part,
    c_send,
    c_recv,
    y_send,
    y_recv,
    mixed,
    mc_recv,
    my_send,
    my_recv,
    mx_send,
    mx_recv,
    acc_z,
    mz_send,
    mz_recv,
    n_ss,
    n_rs,
    x_ss,
    x_rs,
    h_ss,
    h_rs,
    z_ss,
    z_rs,
    c_ss,
    c_rs,
    y_ss,
    y_rs,
    mc_ss,
    mc_rs,
    my_ss,
    my_rs,
    mx_ss,
    mx_rs,
    mz_ss,
    mz_rs,
):
    big_z, big_x, big_y, fan_one, fan_two, hubs_here, halves = sizes
    f32, bf16 = jnp.float32, jnp.bfloat16
    node = lax.axis_index("node")
    feat = lax.axis_index("feat")
    z, x = node // big_x, lax.rem(node, big_x)
    y, core = feat // CORES, lax.rem(feat, CORES)
    x_peers = [{"node": z * big_x + lax.rem(x + o, big_x)} for o in range(1, big_x)]
    z_peers = [{"node": lax.rem(z + o, big_z) * big_x + x} for o in range(1, big_z)]
    y_peers = [{"feat": lax.rem(y + o, big_y) * CORES + core} for o in range(1, big_y)]
    other = 1 - core
    c_peer = {"feat": y * CORES + other}
    shards = big_z * big_x
    n_peers = [{"node": lax.rem(node + o, shards)} for o in range(1, shards)]
    greet(n_peers + y_peers + [c_peer])

    rows, width = table_ref.shape
    front = acc.shape[0]
    reach = tables.shape[1]
    part_width = width // halves

    list_copies = []
    for o, peer in enumerate(n_peers):
        copy = remote(packed_ref, lists.at[node], n_ss.at[o], n_rs.at[o], peer)
        copy.start()
        list_copies.append(copy)
    table_copies = []
    for h in range(halves):
        cut = pl.ds(h * part_width, part_width)
        for o, peer in enumerate(x_peers):
            copy = remote(
                table_ref.at[:, cut],
                tables.at[1 + o, pl.ds(0, rows), cut],
                x_ss.at[h, o],
                x_rs.at[h, o],
                peer,
            )
            copy.start()
            table_copies.append(copy)
        if h == 0:
            for o, peer in enumerate(x_peers):
                copy = remote(
                    hub_ref,
                    tables.at[1 + o, pl.ds(rows, hub_ref.shape[0])],
                    h_ss.at[o],
                    h_rs.at[o],
                    peer,
                )
                copy.start()
                table_copies.append(copy)
    first_copies = 2 * len(x_peers)
    lists[node] = packed_ref[...]
    tail = rows + hub_ref.shape[0]
    tables[0, 0:rows] = table_ref[...]
    tables[0, rows:tail] = hub_ref[...]
    for slot in range(big_x):
        tables[slot, tail:reach] = jnp.zeros((reach - tail, width), bf16)
    for copy in list_copies:
        copy.wait()

    def decode(n, carry):
        entry = lists[n]
        found = jnp.full(entry.shape, -1, jnp.int32)
        for slot in range(big_x):
            owner = z * big_x + lax.rem(x - slot + big_x, big_x)
            feature_at = entry - owner * rows
            hub_at = entry - shards * rows - owner * hubs_here
            found = jnp.where(
                (feature_at >= 0) & (feature_at < rows), feature_at + slot * reach, found
            )
            found = jnp.where(
                (hub_at >= 0) & (hub_at < hubs_here), hub_at + (slot * reach + rows), found
            )
        line = lax.broadcasted_iota(jnp.int32, entry.shape, 0)
        seconds = jnp.clip(entry - node * front, -1, front)
        seconds = jnp.where(line == fan_one + fan_two, entry, seconds)
        local[n] = jnp.where(line < fan_one, found, seconds).T
        return carry

    lax.fori_loop(0, shards, decode, 0)

    def fill(target, at):
        def step(i, carry):
            row0 = pl.multiple_of(i * 32, 32)

            def store(start, value):
                matrix[at, pl.ds(row0, 32), start : start + 128] = value

            count_tiles(local[target, pl.ds(row0, 32), :], fan_one, reach * big_x, store)
            return carry

        lax.fori_loop(0, front // 32, step, 0)

    def sums_of(at, low, high):
        total = jnp.dot(matrix[at, :, 0:reach], tables[0, :, low:high], preferred_element_type=f32)
        for slot in range(1, big_x):
            total = total + jnp.dot(
                matrix[at, :, slot * reach : (slot + 1) * reach],
                tables[slot, :, low:high],
                preferred_element_type=f32,
            )
        return total

    def z_copy(h, s, to):
        peer = {"node": to * big_x + x}
        return remote(z_send.at[h, s], z_recv.at[h, s], z_ss.at[h, s], z_rs.at[h, s], peer)

    slots = matrix.shape[0]
    fill(lax.rem(z + 1, big_z) * big_x + x, 0)
    for copy in table_copies[:first_copies]:
        copy.wait()

    def first_half(s, carry):
        zt = lax.rem(z + 1 + s, big_z)
        at = lax.rem(s, slots)

        @pl.when(s > 0)
        def _():
            fill(zt * big_x + x, at)

        z_send[0, s] = sums_of(at, 0, part_width).astype(bf16)
        z_copy(0, s, zt).start()
        return carry

    lax.fori_loop(0, big_z - 1, first_half, 0)
    for copy in table_copies[first_copies:]:
        copy.wait()
    for h in range(1, halves):

        def other_half(s, carry, h=h):
            z_send[h, s] = sums_of(s, h * part_width, (h + 1) * part_width).astype(bf16)
            z_copy(h, s, lax.rem(z + 1 + s, big_z)).start()
            return carry

        lax.fori_loop(0, big_z - 1, other_half, 0)
    fill(node, 0)
    acc[...] = sums_of(0, 0, width)

    hidden_part = part.shape[2]
    feats = big_y * CORES

    def own_part(f, carry):
        at = pl.ds(pl.multiple_of(f * hidden_part, 128), hidden_part)
        part[f] = jnp.dot(table_ref[0:front, :], self_one[:, at], preferred_element_type=f32)
        return carry

    lax.fori_loop(0, feats, own_part, 0)

    piece = out_ref.shape[0]

    def fill_two(at, carry):
        n, f = at // feats, lax.rem(at, feats)
        zz, xx = n // big_x, lax.rem(n, big_x)
        yy, cc = f // CORES, lax.rem(f, CORES)
        to = (((cc * big_y + yy) * big_x + xx) * big_z + zz) * piece
        from_row = pl.multiple_of(f * piece, 16)
        to_row = pl.multiple_of(to, 16)
        block = local[n, pl.ds(from_row, piece), :]

        def store(start, value):
            matrix_two[pl.ds(to_row, piece), start : start + 128] = value

        count_tiles(block[:, fan_one : fan_one + fan_two], fan_two, front, store)
        weights[pl.ds(to_row, piece), :] = 1.0 / block[
            :, fan_one + fan_two : fan_one + fan_two + 1
        ].astype(f32)
        return carry

    lax.fori_loop(0, shards * feats, fill_two, 0)

    for h in range(halves):
        for s in range(big_z - 1):
            z_copy(h, s, lax.rem(z + 1 + s, big_z)).wait()
            acc[:, h * part_width : (h + 1) * part_width] += z_recv[h, s].astype(f32)
    mean = (acc[...] / counts_ref[...].astype(f32)).astype(bf16)
    means[...] = mean

    def part_of(f):
        at = pl.ds(pl.multiple_of(f * hidden_part, 128), hidden_part)
        return part[f] + jnp.dot(means[...], pool_one[:, at], preferred_element_type=f32)

    def c_copy(s):
        return remote(c_send.at[s], c_recv.at[s], c_ss.at[s], c_rs.at[s], c_peer)

    def c_phase(s, carry):
        yt = lax.rem(y + 1 + s, big_y)
        c_send[s] = part_of(yt * CORES + other)
        c_copy(s).start()
        return carry

    lax.fori_loop(0, big_y, c_phase, 0)

    def y_copy(s, to):
        peer = {"feat": to * CORES + core}
        return remote(y_send.at[s], y_recv.at[s], y_ss.at[s], y_rs.at[s], peer)

    def y_step(s, carry):
        yt = lax.rem(y + 1 + s, big_y)
        total = part_of(yt * CORES + core)
        c_copy(s).wait()
        total = total + c_recv[s]

        @pl.when(s < big_y - 1)
        def _():
            y_send[s] = total.astype(bf16)
            y_copy(s, yt).start()

        @pl.when(s == big_y - 1)
        def _():
            c_send[s] = total

        return carry

    lax.fori_loop(0, big_y, y_step, 0)
    total = c_send[big_y - 1]
    for s in range(big_y - 1):
        y_copy(s, lax.rem(y + 1 + s, big_y)).wait()
        total = total + y_recv[s].astype(f32)
    hidden = jnp.maximum(total, 0.0).astype(bf16)

    projected = jnp.dot(hidden, pool_two[...], preferred_element_type=f32).astype(bf16)
    own = jnp.dot(hidden[0 : piece * feats], self_two[...], preferred_element_type=f32)
    quarter = big_x * big_z * piece
    for c in range(CORES):
        for yy in range(big_y):
            at = (c * big_y + yy) * quarter
            weight = weights[at : at + quarter, :]
            mixed[c, yy] = (
                jnp.dot(matrix_two[at : at + quarter, :], projected, preferred_element_type=f32)
                * weight
            )
            row = pl.multiple_of((x * big_z + z) * piece, 8)
            f = yy * CORES + c
            mixed[c, yy, pl.ds(row, piece), :] += own[f * piece : (f + 1) * piece]

    mc = remote(mixed.at[other], mc_recv, mc_ss, mc_rs, c_peer)
    mc.start()
    mc.wait()
    y_copies = []
    for o in range(big_y - 1):
        yt = lax.rem(y + 1 + o, big_y)
        my_send[o] = (mixed[core, yt] + mc_recv[yt]).astype(bf16)
        copy = remote(my_send.at[o], my_recv.at[o], my_ss.at[o], my_rs.at[o], y_peers[o])
        copy.start()
        y_copies.append(copy)
    total = mixed[core, y] + mc_recv[y]
    for o, copy in enumerate(y_copies):
        copy.wait()
        total = total + my_recv[o].astype(f32)
    mixed[core, y] = total
    slab = big_z * piece
    x_copies = []
    for o in range(big_x - 1):
        row = pl.multiple_of(lax.rem(x + 1 + o, big_x) * slab, 8)
        mx_send[o] = mixed[core, y, pl.ds(row, slab), :].astype(bf16)
        copy = remote(mx_send.at[o], mx_recv.at[o], mx_ss.at[o], mx_rs.at[o], x_peers[o])
        copy.start()
        x_copies.append(copy)
    total = mixed[core, y, pl.ds(pl.multiple_of(x * slab, 8), slab), :]
    for o, copy in enumerate(x_copies):
        copy.wait()
        total = total + mx_recv[o].astype(f32)
    acc_z[...] = total
    mz_send[...] = total.astype(bf16)
    z_copies = []
    for o in range(big_z - 1):
        row = pl.multiple_of(lax.rem(z + 1 + o, big_z) * piece, 16)
        copy = remote(
            mz_send.at[pl.ds(row, piece)], mz_recv.at[o], mz_ss.at[o], mz_rs.at[o], z_peers[o]
        )
        copy.start()
        z_copies.append(copy)
    total = acc_z[pl.ds(pl.multiple_of(z * piece, 8), piece), :]
    for o, copy in enumerate(z_copies):
        copy.wait()
        total = total + mz_recv[o].astype(f32)
    scale = lax.rsqrt(jnp.mean(total * total, axis=1, keepdims=True) + 1e-06)
    out_ref[...] = (total * scale).astype(bf16)


def body(
    feature_table,
    hub_table,
    first_self,
    first_pooled,
    second_self,
    second_pooled,
    first_lists,
    first_counts,
    second_lists,
    second_counts,
):
    shards = lax.axis_size("node")
    feats = lax.axis_size("feat")
    big_x = 2 ** ((shards.bit_length() - 1) // 2)
    big_z = shards // big_x
    big_y = feats // CORES
    rows_here, width = feature_table.shape
    hubs_here = hub_table.shape[0]
    front, fan_one = first_lists.shape
    targets_here, fan_two = second_lists.shape
    piece = targets_here // feats
    out_width = second_self.shape[1]
    hidden_part = second_self.shape[0]

    slots_one = jnp.arange(fan_one, dtype=jnp.int32)[None, :]
    slots_two = jnp.arange(fan_two, dtype=jnp.int32)[None, :]
    lists_one = jnp.where(slots_one < first_counts[:, None], first_lists, -1).T
    lists_two = jnp.where(slots_two < second_counts[:, None], second_lists, -1).T
    lists_two = jnp.concatenate([lists_two, second_counts[None, :]], axis=0)
    lists_two = jnp.pad(lists_two, ((0, 0), (0, front - targets_here)))
    packed = jnp.concatenate([lists_one, lists_two], axis=0)
    hubs = jnp.pad(hub_table, ((0, -hubs_here % 16), (0, 0)))
    reach = rows_here + 128
    halves = 2 if width % 256 == 0 else 1
    bf16, f32 = jnp.bfloat16, jnp.float32
    dma = pltpu.SemaphoreType.DMA
    zs, xs, ys = big_z - 1, big_x - 1, big_y - 1
    quarter = big_x * big_z * piece
    slab = big_z * piece
    block = (front, width)
    hblock = (front, hidden_part)
    vmem = pl.BlockSpec(memory_space=pltpu.VMEM)
    return pl.pallas_call(
        functools.partial(main_kernel, (big_z, big_x, big_y, fan_one, fan_two, hubs_here, halves)),
        out_shape=jax.ShapeDtypeStruct((piece, out_width), bf16),
        in_specs=[vmem] * 8,
        out_specs=vmem,
        scratch_shapes=[
            pltpu.VMEM((shards,) + packed.shape, jnp.int32),
            pltpu.VMEM((shards, front, packed.shape[0]), jnp.int32),
            pltpu.VMEM((big_x, reach, width), bf16),
            pltpu.VMEM((zs if halves > 1 else 1, front, big_x * reach), bf16),
            pltpu.VMEM((targets_here * shards, front), bf16),
            pltpu.VMEM((targets_here * shards, 1), f32),
            pltpu.VMEM(block, bf16),
            pltpu.VMEM(block, f32),
            pltpu.VMEM((halves, zs, front, width // halves), bf16),
            pltpu.VMEM((halves, zs, front, width // halves), bf16),
            pltpu.VMEM((feats,) + hblock, f32),
            pltpu.VMEM((big_y,) + hblock, f32),
            pltpu.VMEM((big_y,) + hblock, f32),
            pltpu.VMEM((ys,) + hblock, bf16),
            pltpu.VMEM((ys,) + hblock, bf16),
            pltpu.VMEM((CORES, big_y, quarter, out_width), f32),
            pltpu.VMEM((big_y, quarter, out_width), f32),
            pltpu.VMEM((ys, quarter, out_width), bf16),
            pltpu.VMEM((ys, quarter, out_width), bf16),
            pltpu.VMEM((xs, slab, out_width), bf16),
            pltpu.VMEM((xs, slab, out_width), bf16),
            pltpu.VMEM((slab, out_width), f32),
            pltpu.VMEM((slab, out_width), bf16),
            pltpu.VMEM((zs, piece, out_width), bf16),
            dma((shards - 1,)),
            dma((shards - 1,)),
            dma((halves, xs)),
            dma((halves, xs)),
            dma((xs,)),
            dma((xs,)),
            dma((halves, zs)),
            dma((halves, zs)),
            dma((big_y,)),
            dma((big_y,)),
            dma((ys,)),
            dma((ys,)),
            dma,
            dma,
            dma((ys,)),
            dma((ys,)),
            dma((xs,)),
            dma((xs,)),
            dma((zs,)),
            dma((zs,)),
        ],
        compiler_params=pltpu.CompilerParams(
            collective_id=1, has_side_effects=True, vmem_limit_bytes=60 * 1024 * 1024
        ),
    )(
        feature_table,
        hubs,
        first_self,
        first_pooled,
        second_self,
        second_pooled,
        packed,
        first_counts[:, None],
    )


def solution(mesh):
    return jax.shard_map(
        body,
        mesh=mesh,
        in_specs=(
            P("node", "feat"),
            P("node", "feat"),
            P("feat", None),
            P("feat", None),
            P("feat", None),
            P("feat", None),
            P("node", None),
            P("node"),
            P("node", None),
            P("node"),
        ),
        out_specs=P(("node", "feat"), None),
        check_vma=False,
    )
```

```python
import functools

import jax
import jax.numpy as jnp
from jax import lax
from jax.experimental import pallas as pl
from jax.experimental.pallas import tpu as pltpu
from jax.sharding import PartitionSpec as P

MESH = pl.DeviceIdType.MESH
CORES = 2


def greet(peers):
    barrier = pltpu.get_barrier_semaphore()
    for peer in peers:
        pl.semaphore_signal(barrier, inc=1, device_id=peer, device_id_type=MESH)
    pl.semaphore_wait(barrier, len(peers))


def remote(src, dst, sends, recvs, peer):
    return pltpu.make_async_remote_copy(
        src_ref=src, dst_ref=dst, send_sem=sends, recv_sem=recvs, device_id=peer, device_id_type=MESH
    )


def count_tiles(local, fan, width, store):
    rows = local.shape[0]
    local = local.astype(jnp.int16)
    one, zero = jnp.bfloat16(1), jnp.bfloat16(0)
    for start in range(0, width, 128):
        columns = (lax.broadcasted_iota(jnp.int32, (rows, 128), 1) + start).astype(jnp.int16)
        total = jnp.zeros((rows, 128), jnp.bfloat16)
        for k in range(fan):
            picked = jnp.broadcast_to(local[:, k : k + 1], (rows, 128))
            total = total + jnp.where(picked == columns, one, zero)
        store(start, total)


def main_kernel(
    sizes,
    table_ref,
    hub_ref,
    self_one,
    pool_one,
    self_two,
    pool_two,
    packed_ref,
    counts_ref,
    out_ref,
    lists,
    local,
    tables,
    matrix,
    matrix_two,
    weights,
    means,
    acc,
    z_send,
    z_recv,
    part,
    c_send,
    c_recv,
    y_send,
    y_recv,
    own_ref,
    mixed,
    mc_send,
    mc_recv,
    my_send,
    my_recv,
    mx_send,
    mx_recv,
    acc_z,
    mz_send,
    mz_recv,
    n_ss,
    n_rs,
    x_ss,
    x_rs,
    h_ss,
    h_rs,
    z_ss,
    z_rs,
    c_ss,
    c_rs,
    y_ss,
    y_rs,
    mc_ss,
    mc_rs,
    my_ss,
    my_rs,
    mx_ss,
    mx_rs,
    mz_ss,
    mz_rs,
):
    big_z, big_x, big_y, fan_one, fan_two, hubs_here, edges = sizes
    f32, bf16 = jnp.float32, jnp.bfloat16
    node = lax.axis_index("node")
    feat = lax.axis_index("feat")
    z, x = node // big_x, lax.rem(node, big_x)
    y, core = feat // CORES, lax.rem(feat, CORES)
    x_peers = [{"node": z * big_x + lax.rem(x + o, big_x)} for o in range(1, big_x)]
    z_peers = [{"node": lax.rem(z + o, big_z) * big_x + x} for o in range(1, big_z)]
    y_peers = [{"feat": lax.rem(y + o, big_y) * CORES + core} for o in range(1, big_y)]
    other = 1 - core
    c_peer = {"feat": y * CORES + other}
    shards = big_z * big_x
    n_peers = [{"node": lax.rem(node + o, shards)} for o in range(1, shards)]
    greet(n_peers + y_peers + [c_peer])

    rows, width = table_ref.shape
    front = acc.shape[0]
    reach = tables.shape[1]
    halves = len(edges) - 1

    list_copies = []
    for o, peer in enumerate(n_peers):
        copy = remote(packed_ref, lists.at[node], n_ss.at[o], n_rs.at[o], peer)
        copy.start()
        list_copies.append(copy)
    table_copies = []
    for h in range(halves):
        cut = pl.ds(edges[h], edges[h + 1] - edges[h])
        for o, peer in enumerate(x_peers):
            copy = remote(
                table_ref.at[:, cut],
                tables.at[1 + o, pl.ds(0, rows), cut],
                x_ss.at[h, o],
                x_rs.at[h, o],
                peer,
            )
            copy.start()
            table_copies.append(copy)
        if h == 0:
            for o, peer in enumerate(x_peers):
                copy = remote(
                    hub_ref,
                    tables.at[1 + o, pl.ds(rows, hub_ref.shape[0])],
                    h_ss.at[o],
                    h_rs.at[o],
                    peer,
                )
                copy.start()
                table_copies.append(copy)
    first_copies = 2 * len(x_peers)
    lists[node] = packed_ref[...]
    tail = rows + hub_ref.shape[0]
    tables[0, 0:rows] = table_ref[...]
    tables[0, rows:tail] = hub_ref[...]
    for slot in range(big_x):
        tables[slot, tail:reach] = jnp.zeros((reach - tail, width), bf16)
    for copy in list_copies:
        copy.wait()

    def decode(n, carry):
        entry = lists[n]
        found = jnp.full(entry.shape, -1, jnp.int32)
        for slot in range(big_x):
            owner = z * big_x + lax.rem(x - slot + big_x, big_x)
            feature_at = entry - owner * rows
            hub_at = entry - shards * rows - owner * hubs_here
            found = jnp.where(
                (feature_at >= 0) & (feature_at < rows), feature_at + slot * reach, found
            )
            found = jnp.where(
                (hub_at >= 0) & (hub_at < hubs_here), hub_at + (slot * reach + rows), found
            )
        line = lax.broadcasted_iota(jnp.int32, entry.shape, 0)
        seconds = jnp.clip(entry - node * front, -1, front)
        seconds = jnp.where(line == fan_one + fan_two, entry, seconds)
        local[n] = jnp.where(line < fan_one, found, seconds).T
        return carry

    lax.fori_loop(0, shards, decode, 0)

    def fill(target, at):
        def step(i, carry):
            row0 = pl.multiple_of(i * 32, 32)

            def store(start, value):
                matrix[at, pl.ds(row0, 32), start : start + 128] = value

            count_tiles(local[target, pl.ds(row0, 32), :], fan_one, reach * big_x, store)
            return carry

        lax.fori_loop(0, front // 32, step, 0)

    def sums_of(at, low, high):
        total = jnp.dot(matrix[at, :, 0:reach], tables[0, :, low:high], preferred_element_type=f32)
        for slot in range(1, big_x):
            total = total + jnp.dot(
                matrix[at, :, slot * reach : (slot + 1) * reach],
                tables[slot, :, low:high],
                preferred_element_type=f32,
            )
        return total

    def z_copy(h, s, to):
        peer = {"node": to * big_x + x}
        cut = pl.ds(edges[h], edges[h + 1] - edges[h])
        return remote(
            z_send.at[s, :, cut], z_recv.at[s, :, cut], z_ss.at[h, s], z_rs.at[h, s], peer
        )

    slots = matrix.shape[0]
    fill(lax.rem(z + 1, big_z) * big_x + x, 0)
    for copy in table_copies[:first_copies]:
        copy.wait()

    def first_half(s, carry):
        zt = lax.rem(z + 1 + s, big_z)
        at = lax.rem(s, slots)

        @pl.when(s > 0)
        def _():
            fill(zt * big_x + x, at)

        z_send[s, :, 0 : edges[1]] = sums_of(at, 0, edges[1]).astype(bf16)
        z_copy(0, s, zt).start()
        return carry

    lax.fori_loop(0, big_z - 1, first_half, 0)
    for h in range(1, halves):
        begin = first_copies + (h - 1) * len(x_peers)
        for copy in table_copies[begin : begin + len(x_peers)]:
            copy.wait()

        def other_half(s, carry, h=h):
            low, high = edges[h], edges[h + 1]
            z_send[s, :, low:high] = sums_of(s, low, high).astype(bf16)
            z_copy(h, s, lax.rem(z + 1 + s, big_z)).start()
            return carry

        lax.fori_loop(0, big_z - 1, other_half, 0)
    fill(node, 0)
    acc[...] = sums_of(0, 0, width)

    hidden_part = part.shape[2]
    feats = big_y * CORES

    def own_part(f, carry):
        at = pl.ds(pl.multiple_of(f * hidden_part, 128), hidden_part)
        part[f] = jnp.dot(table_ref[0:front, :], self_one[:, at], preferred_element_type=f32)
        return carry

    lax.fori_loop(0, feats, own_part, 0)

    piece = out_ref.shape[0]

    def fill_two(at, carry):
        n, f = at // feats, lax.rem(at, feats)
        zz, xx = n // big_x, lax.rem(n, big_x)
        yy, cc = f // CORES, lax.rem(f, CORES)
        to = (((cc * big_y + yy) * big_x + xx) * big_z + zz) * piece
        from_row = pl.multiple_of(f * piece, 16)
        to_row = pl.multiple_of(to, 16)
        block = local[n, pl.ds(from_row, piece), :]

        def store(start, value):
            matrix_two[pl.ds(to_row, piece), start : start + 128] = value

        count_tiles(block[:, fan_one : fan_one + fan_two], fan_two, front, store)
        weights[pl.ds(to_row, piece), :] = 1.0 / block[
            :, fan_one + fan_two : fan_one + fan_two + 1
        ].astype(f32)
        return carry

    lax.fori_loop(0, shards * feats, fill_two, 0)

    for h in range(halves):
        for s in range(big_z - 1):
            z_copy(h, s, lax.rem(z + 1 + s, big_z)).wait()
            low, high = edges[h], edges[h + 1]
            acc[:, low:high] += z_recv[s, :, low:high].astype(f32)
    mean = (acc[...] / counts_ref[...].astype(f32)).astype(bf16)
    means[...] = mean

    def part_of(f):
        at = pl.ds(pl.multiple_of(f * hidden_part, 128), hidden_part)
        return part[f] + jnp.dot(means[...], pool_one[:, at], preferred_element_type=f32)

    def c_copy(s):
        return remote(c_send.at[s], c_recv.at[s], c_ss.at[s], c_rs.at[s], c_peer)

    def c_phase(s, carry):
        yt = lax.rem(y + 1 + s, big_y)
        c_send[s] = part_of(yt * CORES + other)
        c_copy(s).start()
        return carry

    lax.fori_loop(0, big_y, c_phase, 0)

    def y_copy(s, to):
        peer = {"feat": to * CORES + core}
        return remote(y_send.at[s], y_recv.at[s], y_ss.at[s], y_rs.at[s], peer)

    def y_step(s, carry):
        yt = lax.rem(y + 1 + s, big_y)
        total = part_of(yt * CORES + core)
        c_copy(s).wait()
        total = total + c_recv[s]

        @pl.when(s < big_y - 1)
        def _():
            y_send[s] = total.astype(bf16)
            y_copy(s, yt).start()

        @pl.when(s == big_y - 1)
        def _():
            c_send[s] = total

        return carry

    lax.fori_loop(0, big_y, y_step, 0)
    total = c_send[big_y - 1]
    for s in range(big_y - 1):
        y_copy(s, lax.rem(y + 1 + s, big_y)).wait()
        total = total + y_recv[s].astype(f32)
    hidden = jnp.maximum(total, 0.0).astype(bf16)

    projected = jnp.dot(hidden, pool_two[...], preferred_element_type=f32).astype(bf16)
    own_ref[...] = jnp.dot(hidden[0 : piece * feats], self_two[...], preferred_element_type=f32)
    quarter = big_x * big_z * piece
    slab = big_z * piece

    def mix(k, s, c, yy):
        at = pl.ds(pl.multiple_of((c * big_y + yy) * quarter, 16), quarter)
        mixed[k, s] = (
            jnp.dot(matrix_two[at, :], projected, preferred_element_type=f32) * weights[at, :]
        )
        row = pl.multiple_of((x * big_z + z) * piece, 16)
        from_row = pl.multiple_of((yy * CORES + c) * piece, 16)
        mixed[k, s, pl.ds(row, piece), :] += own_ref[pl.ds(from_row, piece), :]

    core_copies = []
    for s in range(big_y):
        mix(0, s, other, lax.rem(y + 1 + s, big_y))
        mc_send[s] = mixed[0, s].astype(bf16)
        copy = remote(mc_send.at[s], mc_recv.at[s], mc_ss.at[s], mc_rs.at[s], c_peer)
        copy.start()
        core_copies.append(copy)
    for s in range(big_y):
        mix(1, s, core, lax.rem(y + 1 + s, big_y))
    x_rows = [
        pl.ds(pl.multiple_of(lax.rem(x + 1 + o, big_x) * slab, 16), slab) for o in range(big_x)
    ]
    y_copies = {}
    for s in range(big_y):
        core_copies[s].wait()
        mixed[1, s] += mc_recv[s].astype(f32)
        if s < big_y - 1:
            for o in range(big_x):
                my_send[s, o] = mixed[1, s, x_rows[o], :].astype(bf16)
                copy = remote(
                    my_send.at[s, o], my_recv.at[s, o], my_ss.at[s, o], my_rs.at[s, o], y_peers[s]
                )
                copy.start()
                y_copies[s, o] = copy
    x_copies = []
    for o in range(big_x):
        total = mixed[1, big_y - 1, x_rows[o], :]
        for s in range(big_y - 1):
            y_copies[s, o].wait()
            total = total + my_recv[s, o].astype(f32)
        if o < big_x - 1:
            mx_send[o] = total.astype(bf16)
            copy = remote(mx_send.at[o], mx_recv.at[o], mx_ss.at[o], mx_rs.at[o], x_peers[o])
            copy.start()
            x_copies.append(copy)
    for o, copy in enumerate(x_copies):
        copy.wait()
        total = total + mx_recv[o].astype(f32)
    acc_z[...] = total
    mz_send[...] = total.astype(bf16)
    z_copies = []
    for o in range(big_z - 1):
        row = pl.multiple_of(lax.rem(z + 1 + o, big_z) * piece, 16)
        copy = remote(
            mz_send.at[pl.ds(row, piece)], mz_recv.at[o], mz_ss.at[o], mz_rs.at[o], z_peers[o]
        )
        copy.start()
        z_copies.append(copy)
    total = acc_z[pl.ds(pl.multiple_of(z * piece, 8), piece), :]
    for o, copy in enumerate(z_copies):
        copy.wait()
        total = total + mz_recv[o].astype(f32)
    scale = lax.rsqrt(jnp.mean(total * total, axis=1, keepdims=True) + 1e-06)
    out_ref[...] = (total * scale).astype(bf16)


def body(
    feature_table,
    hub_table,
    first_self,
    first_pooled,
    second_self,
    second_pooled,
    first_lists,
    first_counts,
    second_lists,
    second_counts,
):
    shards = lax.axis_size("node")
    feats = lax.axis_size("feat")
    big_x = 2 ** ((shards.bit_length() - 1) // 2)
    big_z = shards // big_x
    big_y = feats // CORES
    rows_here, width = feature_table.shape
    hubs_here = hub_table.shape[0]
    front, fan_one = first_lists.shape
    targets_here, fan_two = second_lists.shape
    piece = targets_here // feats
    out_width = second_self.shape[1]
    hidden_part = second_self.shape[0]

    slots_one = jnp.arange(fan_one, dtype=jnp.int32)[None, :]
    slots_two = jnp.arange(fan_two, dtype=jnp.int32)[None, :]
    lists_one = jnp.where(slots_one < first_counts[:, None], first_lists, -1).T
    lists_two = jnp.where(slots_two < second_counts[:, None], second_lists, -1).T
    lists_two = jnp.concatenate([lists_two, second_counts[None, :]], axis=0)
    lists_two = jnp.pad(lists_two, ((0, 0), (0, front - targets_here)))
    packed = jnp.concatenate([lists_one, lists_two], axis=0)
    hubs = jnp.pad(hub_table, ((0, -hubs_here % 16), (0, 0)))
    reach = rows_here + 128
    edges = (0, 128, 256, width) if width > 256 else (0, width)
    halves = len(edges) - 1
    bf16, f32 = jnp.bfloat16, jnp.float32
    dma = pltpu.SemaphoreType.DMA
    zs, xs, ys = big_z - 1, big_x - 1, big_y - 1
    quarter = big_x * big_z * piece
    slab = big_z * piece
    block = (front, width)
    hblock = (front, hidden_part)
    vmem = pl.BlockSpec(memory_space=pltpu.VMEM)
    return pl.pallas_call(
        functools.partial(main_kernel, (big_z, big_x, big_y, fan_one, fan_two, hubs_here, edges)),
        out_shape=jax.ShapeDtypeStruct((piece, out_width), bf16),
        in_specs=[vmem] * 8,
        out_specs=vmem,
        scratch_shapes=[
            pltpu.VMEM((shards,) + packed.shape, jnp.int32),
            pltpu.VMEM((shards, front, packed.shape[0]), jnp.int32),
            pltpu.VMEM((big_x, reach, width), bf16),
            pltpu.VMEM((zs if halves > 1 else 1, front, big_x * reach), bf16),
            pltpu.VMEM((targets_here * shards, front), bf16),
            pltpu.VMEM((targets_here * shards, 1), f32),
            pltpu.VMEM(block, bf16),
            pltpu.VMEM(block, f32),
            pltpu.VMEM((zs,) + block, bf16),
            pltpu.VMEM((zs,) + block, bf16),
            pltpu.VMEM((feats,) + hblock, f32),
            pltpu.VMEM((big_y,) + hblock, f32),
            pltpu.VMEM((big_y,) + hblock, f32),
            pltpu.VMEM((ys,) + hblock, bf16),
            pltpu.VMEM((ys,) + hblock, bf16),
            pltpu.VMEM((targets_here, out_width), f32),
            pltpu.VMEM((CORES, big_y, quarter, out_width), f32),
            pltpu.VMEM((big_y, quarter, out_width), bf16),
            pltpu.VMEM((big_y, quarter, out_width), bf16),
            pltpu.VMEM((ys, big_x, slab, out_width), bf16),
            pltpu.VMEM((ys, big_x, slab, out_width), bf16),
            pltpu.VMEM((xs, slab, out_width), bf16),
            pltpu.VMEM((xs, slab, out_width), bf16),
            pltpu.VMEM((slab, out_width), f32),
            pltpu.VMEM((slab, out_width), bf16),
            pltpu.VMEM((zs, piece, out_width), bf16),
            dma((shards - 1,)),
            dma((shards - 1,)),
            dma((halves, xs)),
            dma((halves, xs)),
            dma((xs,)),
            dma((xs,)),
            dma((halves, zs)),
            dma((halves, zs)),
            dma((big_y,)),
            dma((big_y,)),
            dma((ys,)),
            dma((ys,)),
            dma((big_y,)),
            dma((big_y,)),
            dma((ys, big_x)),
            dma((ys, big_x)),
            dma((xs,)),
            dma((xs,)),
            dma((zs,)),
            dma((zs,)),
        ],
        compiler_params=pltpu.CompilerParams(
            collective_id=1, has_side_effects=True, vmem_limit_bytes=60 * 1024 * 1024
        ),
    )(
        feature_table,
        hubs,
        first_self,
        first_pooled,
        second_self,
        second_pooled,
        packed,
        first_counts[:, None],
    )


def solution(mesh):
    return jax.shard_map(
        body,
        mesh=mesh,
        in_specs=(
            P("node", "feat"),
            P("node", "feat"),
            P("feat", None),
            P("feat", None),
            P("feat", None),
            P("feat", None),
            P("node", None),
            P("node"),
            P("node", None),
            P("node"),
        ),
        out_specs=P(("node", "feat"), None),
        check_vma=False,
    )
```

```python
import functools

import jax
import jax.numpy as jnp
from jax import lax
from jax.experimental import pallas as pl
from jax.experimental.pallas import tpu as pltpu
from jax.sharding import PartitionSpec as P

MESH = pl.DeviceIdType.MESH
CORES = 2


def greet(peers):
    barrier = pltpu.get_barrier_semaphore()
    for peer in peers:
        pl.semaphore_signal(barrier, inc=1, device_id=peer, device_id_type=MESH)
    pl.semaphore_wait(barrier, len(peers))


def remote(src, dst, sends, recvs, peer):
    return pltpu.make_async_remote_copy(
        src_ref=src, dst_ref=dst, send_sem=sends, recv_sem=recvs, device_id=peer, device_id_type=MESH
    )


def count_tiles(local, fan, width, store):
    rows = local.shape[0]
    local = local.astype(jnp.int16)
    one, zero = jnp.bfloat16(1), jnp.bfloat16(0)
    for start in range(0, width, 128):
        columns = (lax.broadcasted_iota(jnp.int32, (rows, 128), 1) + start).astype(jnp.int16)
        total = jnp.zeros((rows, 128), jnp.bfloat16)
        for k in range(fan):
            picked = jnp.broadcast_to(local[:, k : k + 1], (rows, 128))
            total = total + jnp.where(picked == columns, one, zero)
        store(start, total)


def main_kernel(
    sizes,
    table_ref,
    hub_ref,
    self_one,
    pool_one,
    self_two,
    pool_two,
    packed_ref,
    counts_ref,
    out_ref,
    lists,
    local,
    tables,
    matrix,
    matrix_two,
    weights,
    means,
    acc,
    z_send,
    z_recv,
    part,
    c_send,
    c_recv,
    y_send,
    y_recv,
    own_ref,
    mixed,
    mc_send,
    mc_recv,
    my_send,
    my_recv,
    mx_send,
    mx_recv,
    acc_z,
    mz_send,
    mz_recv,
    n_ss,
    n_rs,
    x_ss,
    x_rs,
    h_ss,
    h_rs,
    z_ss,
    z_rs,
    c_ss,
    c_rs,
    y_ss,
    y_rs,
    mc_ss,
    mc_rs,
    my_ss,
    my_rs,
    mx_ss,
    mx_rs,
    mz_ss,
    mz_rs,
):
    big_z, big_x, big_y, fan_one, fan_two, hubs_here, edges = sizes
    f32, bf16 = jnp.float32, jnp.bfloat16
    node = lax.axis_index("node")
    feat = lax.axis_index("feat")
    z, x = node // big_x, lax.rem(node, big_x)
    y, core = feat // CORES, lax.rem(feat, CORES)
    x_peers = [{"node": z * big_x + lax.rem(x + o, big_x)} for o in range(1, big_x)]
    z_peers = [{"node": lax.rem(z + o, big_z) * big_x + x} for o in range(1, big_z)]
    y_peers = [{"feat": lax.rem(y + o, big_y) * CORES + core} for o in range(1, big_y)]
    other = 1 - core
    c_peer = {"feat": y * CORES + other}
    shards = big_z * big_x
    n_peers = [{"node": lax.rem(node + o, shards)} for o in range(1, shards)]
    greet(n_peers + y_peers + [c_peer])

    rows, width = table_ref.shape
    front = acc.shape[0]
    reach = tables.shape[1]
    halves = len(edges) - 1

    list_copies = []
    for o, peer in enumerate(n_peers):
        copy = remote(packed_ref, lists.at[node], n_ss.at[o], n_rs.at[o], peer)
        copy.start()
        list_copies.append(copy)
    table_copies = []
    for h in range(halves):
        cut = pl.ds(edges[h], edges[h + 1] - edges[h])
        for o, peer in enumerate(x_peers):
            copy = remote(
                table_ref.at[:, cut],
                tables.at[1 + o, pl.ds(0, rows), cut],
                x_ss.at[h, o],
                x_rs.at[h, o],
                peer,
            )
            copy.start()
            table_copies.append(copy)
        if h == 0:
            for o, peer in enumerate(x_peers):
                copy = remote(
                    hub_ref,
                    tables.at[1 + o, pl.ds(rows, hub_ref.shape[0])],
                    h_ss.at[o],
                    h_rs.at[o],
                    peer,
                )
                copy.start()
                table_copies.append(copy)
    first_copies = 2 * len(x_peers)
    lists[node] = packed_ref[...]
    tail = rows + hub_ref.shape[0]
    tables[0, 0:rows] = table_ref[...]
    tables[0, rows:tail] = hub_ref[...]
    for slot in range(big_x):
        tables[slot, tail:reach] = jnp.zeros((reach - tail, width), bf16)
    for copy in list_copies:
        copy.wait()

    def decode(n, carry):
        entry = lists[n]
        found = jnp.full(entry.shape, -1, jnp.int32)
        for slot in range(big_x):
            owner = z * big_x + lax.rem(x - slot + big_x, big_x)
            feature_at = entry - owner * rows
            hub_at = entry - shards * rows - owner * hubs_here
            found = jnp.where(
                (feature_at >= 0) & (feature_at < rows), feature_at + slot * reach, found
            )
            found = jnp.where(
                (hub_at >= 0) & (hub_at < hubs_here), hub_at + (slot * reach + rows), found
            )
        line = lax.broadcasted_iota(jnp.int32, entry.shape, 0)
        seconds = jnp.clip(entry - node * front, -1, front)
        seconds = jnp.where(line == fan_one + fan_two, entry, seconds)
        local[n] = jnp.where(line < fan_one, found, seconds).T
        return carry

    lax.fori_loop(0, shards, decode, 0)

    def fill(target, at):
        def step(i, carry):
            row0 = pl.multiple_of(i * 32, 32)

            def store(start, value):
                matrix[at, pl.ds(row0, 32), start : start + 128] = value

            count_tiles(local[target, pl.ds(row0, 32), :], fan_one, reach * big_x, store)
            return carry

        lax.fori_loop(0, front // 32, step, 0)

    def sums_of(at, top, deep, low, high):
        total = jnp.dot(matrix[at, top : top + deep, 0:reach], tables[0, :, low:high], preferred_element_type=f32)
        for slot in range(1, big_x):
            total = total + jnp.dot(
                matrix[at, top : top + deep, slot * reach : (slot + 1) * reach],
                tables[slot, :, low:high],
                preferred_element_type=f32,
            )
        return total

    half = front // 2
    pieces = [(h, 0, front, edges[h], edges[h + 1]) for h in range(halves)]
    if halves > 1:
        last = pieces.pop()
        pieces += [(last[0], r * half, half, last[3], last[4]) for r in range(2)]

    def z_copy(p, s, to):
        peer = {"node": to * big_x + x}
        _, top, deep, low, high = pieces[p]
        at = (s, pl.ds(top, deep), pl.ds(low, high - low))
        return remote(z_send.at[at], z_recv.at[at], z_ss.at[p, s], z_rs.at[p, s], peer)

    slots = matrix.shape[0]
    fill(lax.rem(z + 1, big_z) * big_x + x, 0)
    for copy in table_copies[:first_copies]:
        copy.wait()

    def first_half(s, carry):
        zt = lax.rem(z + 1 + s, big_z)
        at = lax.rem(s, slots)

        @pl.when(s > 0)
        def _():
            fill(zt * big_x + x, at)

        z_send[s, :, 0 : edges[1]] = sums_of(at, 0, front, 0, edges[1]).astype(bf16)
        z_copy(0, s, zt).start()
        return carry

    lax.fori_loop(0, big_z - 1, first_half, 0)
    for p in range(1, len(pieces)):
        h, top, deep, low, high = pieces[p]
        if top == 0:
            begin = first_copies + (h - 1) * len(x_peers)
            for copy in table_copies[begin : begin + len(x_peers)]:
                copy.wait()

        def other_piece(s, carry, p=p, top=top, deep=deep, low=low, high=high):
            z_send[s, top : top + deep, low:high] = sums_of(s, top, deep, low, high).astype(bf16)
            z_copy(p, s, lax.rem(z + 1 + s, big_z)).start()
            return carry

        lax.fori_loop(0, big_z - 1, other_piece, 0)
    fill(node, 0)
    acc[...] = sums_of(0, 0, front, 0, width)

    hidden_part = part.shape[2]
    feats = big_y * CORES

    def own_part(f, carry):
        at = pl.ds(pl.multiple_of(f * hidden_part, 128), hidden_part)
        part[f] = jnp.dot(table_ref[0:front, :], self_one[:, at], preferred_element_type=f32)
        return carry

    lax.fori_loop(0, feats, own_part, 0)

    piece = out_ref.shape[0]

    def fill_two(at, carry):
        n, f = at // feats, lax.rem(at, feats)
        zz, xx = n // big_x, lax.rem(n, big_x)
        yy, cc = f // CORES, lax.rem(f, CORES)
        to = (((cc * big_y + yy) * big_x + xx) * big_z + zz) * piece
        from_row = pl.multiple_of(f * piece, 16)
        to_row = pl.multiple_of(to, 16)
        block = local[n, pl.ds(from_row, piece), :]

        def store(start, value):
            matrix_two[pl.ds(to_row, piece), start : start + 128] = value

        count_tiles(block[:, fan_one : fan_one + fan_two], fan_two, front, store)
        weights[pl.ds(to_row, piece), :] = 1.0 / block[
            :, fan_one + fan_two : fan_one + fan_two + 1
        ].astype(f32)
        return carry

    lax.fori_loop(0, shards * feats, fill_two, 0)

    def c_copy(r, s):
        at = (s, pl.ds(r * half, half))
        return remote(c_send.at[at], c_recv.at[at], c_ss.at[r, s], c_rs.at[r, s], c_peer)

    def y_copy(r, s, to):
        peer = {"feat": to * CORES + core}
        at = (s, pl.ds(r * half, half))
        return remote(y_send.at[at], y_recv.at[at], y_ss.at[r, s], y_rs.at[r, s], peer)

    for r in range(2):
        top, end = r * half, (r + 1) * half
        for p, (_, first, deep, low, high) in enumerate(pieces):
            if first == top:
                for s in range(big_z - 1):
                    z_copy(p, s, lax.rem(z + 1 + s, big_z)).wait()
                    acc[first : first + deep, low:high] += z_recv[
                        s, first : first + deep, low:high
                    ].astype(f32)
        means[top:end, :] = (acc[top:end, :] / counts_ref[top:end, :].astype(f32)).astype(bf16)

        def part_of(f, top=top, end=end):
            at = pl.ds(pl.multiple_of(f * hidden_part, 128), hidden_part)
            return part[f, top:end, :] + jnp.dot(
                means[top:end, :], pool_one[:, at], preferred_element_type=f32
            )

        def c_phase(s, carry, r=r, top=top, end=end, part_of=part_of):
            yt = lax.rem(y + 1 + s, big_y)
            c_send[s, top:end, :] = part_of(yt * CORES + other)
            c_copy(r, s).start()
            return carry

        lax.fori_loop(0, big_y, c_phase, 0)

        def y_step(s, carry, r=r, top=top, end=end, part_of=part_of):
            yt = lax.rem(y + 1 + s, big_y)
            total = part_of(yt * CORES + core)
            c_copy(r, s).wait()
            total = total + c_recv[s, top:end, :]

            @pl.when(s < big_y - 1)
            def _():
                y_send[s, top:end, :] = total.astype(bf16)
                y_copy(r, s, yt).start()

            @pl.when(s == big_y - 1)
            def _():
                c_send[s, top:end, :] = total

            return carry

        lax.fori_loop(0, big_y, y_step, 0)
    total = c_send[big_y - 1]
    for s in range(big_y - 1):
        for r in range(2):
            y_copy(r, s, lax.rem(y + 1 + s, big_y)).wait()
        total = total + y_recv[s].astype(f32)
    hidden = jnp.maximum(total, 0.0).astype(bf16)

    projected = jnp.dot(hidden, pool_two[...], preferred_element_type=f32).astype(bf16)
    own_ref[...] = jnp.dot(hidden[0 : piece * feats], self_two[...], preferred_element_type=f32)
    quarter = big_x * big_z * piece
    slab = big_z * piece

    def mix(k, s, c, yy):
        at = pl.ds(pl.multiple_of((c * big_y + yy) * quarter, 16), quarter)
        mixed[k, s] = (
            jnp.dot(matrix_two[at, :], projected, preferred_element_type=f32) * weights[at, :]
        )
        row = pl.multiple_of((x * big_z + z) * piece, 16)
        from_row = pl.multiple_of((yy * CORES + c) * piece, 16)
        mixed[k, s, pl.ds(row, piece), :] += own_ref[pl.ds(from_row, piece), :]

    core_copies = []
    for s in range(big_y):
        mix(0, s, other, lax.rem(y + 1 + s, big_y))
        mc_send[s] = mixed[0, s].astype(bf16)
        copy = remote(mc_send.at[s], mc_recv.at[s], mc_ss.at[s], mc_rs.at[s], c_peer)
        copy.start()
        core_copies.append(copy)
    for s in range(big_y):
        mix(1, s, core, lax.rem(y + 1 + s, big_y))
    x_rows = [
        pl.ds(pl.multiple_of(lax.rem(x + 1 + o, big_x) * slab, 16), slab) for o in range(big_x)
    ]
    y_copies = {}
    for s in range(big_y):
        core_copies[s].wait()
        mixed[1, s] += mc_recv[s].astype(f32)
        if s < big_y - 1:
            for o in range(big_x):
                my_send[s, o] = mixed[1, s, x_rows[o], :].astype(bf16)
                copy = remote(
                    my_send.at[s, o], my_recv.at[s, o], my_ss.at[s, o], my_rs.at[s, o], y_peers[s]
                )
                copy.start()
                y_copies[s, o] = copy
    x_copies = []
    for o in range(big_x):
        total = mixed[1, big_y - 1, x_rows[o], :]
        for s in range(big_y - 1):
            y_copies[s, o].wait()
            total = total + my_recv[s, o].astype(f32)
        if o < big_x - 1:
            mx_send[o] = total.astype(bf16)
            copy = remote(mx_send.at[o], mx_recv.at[o], mx_ss.at[o], mx_rs.at[o], x_peers[o])
            copy.start()
            x_copies.append(copy)
    for o, copy in enumerate(x_copies):
        copy.wait()
        total = total + mx_recv[o].astype(f32)
    acc_z[...] = total
    mz_send[...] = total.astype(bf16)
    z_copies = []
    for o in range(big_z - 1):
        row = pl.multiple_of(lax.rem(z + 1 + o, big_z) * piece, 16)
        copy = remote(
            mz_send.at[pl.ds(row, piece)], mz_recv.at[o], mz_ss.at[o], mz_rs.at[o], z_peers[o]
        )
        copy.start()
        z_copies.append(copy)
    total = acc_z[pl.ds(pl.multiple_of(z * piece, 8), piece), :]
    for o, copy in enumerate(z_copies):
        copy.wait()
        total = total + mz_recv[o].astype(f32)
    scale = lax.rsqrt(jnp.mean(total * total, axis=1, keepdims=True) + 1e-06)
    out_ref[...] = (total * scale).astype(bf16)


def body(
    feature_table,
    hub_table,
    first_self,
    first_pooled,
    second_self,
    second_pooled,
    first_lists,
    first_counts,
    second_lists,
    second_counts,
):
    shards = lax.axis_size("node")
    feats = lax.axis_size("feat")
    big_x = 2 ** ((shards.bit_length() - 1) // 2)
    big_z = shards // big_x
    big_y = feats // CORES
    rows_here, width = feature_table.shape
    hubs_here = hub_table.shape[0]
    front, fan_one = first_lists.shape
    targets_here, fan_two = second_lists.shape
    piece = targets_here // feats
    out_width = second_self.shape[1]
    hidden_part = second_self.shape[0]

    slots_one = jnp.arange(fan_one, dtype=jnp.int32)[None, :]
    slots_two = jnp.arange(fan_two, dtype=jnp.int32)[None, :]
    lists_one = jnp.where(slots_one < first_counts[:, None], first_lists, -1).T
    lists_two = jnp.where(slots_two < second_counts[:, None], second_lists, -1).T
    lists_two = jnp.concatenate([lists_two, second_counts[None, :]], axis=0)
    lists_two = jnp.pad(lists_two, ((0, 0), (0, front - targets_here)))
    packed = jnp.concatenate([lists_one, lists_two], axis=0)
    hubs = jnp.pad(hub_table, ((0, -hubs_here % 16), (0, 0)))
    reach = rows_here + 128
    edges = (0, 128, 256, width) if width > 256 else (0, width)
    chunks = len(edges) if len(edges) > 2 else 1
    bf16, f32 = jnp.bfloat16, jnp.float32
    dma = pltpu.SemaphoreType.DMA
    zs, xs, ys = big_z - 1, big_x - 1, big_y - 1
    quarter = big_x * big_z * piece
    slab = big_z * piece
    block = (front, width)
    hblock = (front, hidden_part)
    vmem = pl.BlockSpec(memory_space=pltpu.VMEM)
    return pl.pallas_call(
        functools.partial(main_kernel, (big_z, big_x, big_y, fan_one, fan_two, hubs_here, edges)),
        out_shape=jax.ShapeDtypeStruct((piece, out_width), bf16),
        in_specs=[vmem] * 8,
        out_specs=vmem,
        scratch_shapes=[
            pltpu.VMEM((shards,) + packed.shape, jnp.int32),
            pltpu.VMEM((shards, front, packed.shape[0]), jnp.int32),
            pltpu.VMEM((big_x, reach, width), bf16),
            pltpu.VMEM((zs if chunks > 1 else 1, front, big_x * reach), bf16),
            pltpu.VMEM((targets_here * shards, front), bf16),
            pltpu.VMEM((targets_here * shards, 1), f32),
            pltpu.VMEM(block, bf16),
            pltpu.VMEM(block, f32),
            pltpu.VMEM((zs,) + block, bf16),
            pltpu.VMEM((zs,) + block, bf16),
            pltpu.VMEM((feats,) + hblock, f32),
            pltpu.VMEM((big_y,) + hblock, f32),
            pltpu.VMEM((big_y,) + hblock, f32),
            pltpu.VMEM((ys,) + hblock, bf16),
            pltpu.VMEM((ys,) + hblock, bf16),
            pltpu.VMEM((targets_here, out_width), f32),
            pltpu.VMEM((CORES, big_y, quarter, out_width), f32),
            pltpu.VMEM((big_y, quarter, out_width), bf16),
            pltpu.VMEM((big_y, quarter, out_width), bf16),
            pltpu.VMEM((ys, big_x, slab, out_width), bf16),
            pltpu.VMEM((ys, big_x, slab, out_width), bf16),
            pltpu.VMEM((xs, slab, out_width), bf16),
            pltpu.VMEM((xs, slab, out_width), bf16),
            pltpu.VMEM((slab, out_width), f32),
            pltpu.VMEM((slab, out_width), bf16),
            pltpu.VMEM((zs, piece, out_width), bf16),
            dma((shards - 1,)),
            dma((shards - 1,)),
            dma((len(edges) - 1, xs)),
            dma((len(edges) - 1, xs)),
            dma((xs,)),
            dma((xs,)),
            dma((chunks, zs)),
            dma((chunks, zs)),
            dma((2, big_y)),
            dma((2, big_y)),
            dma((2, ys)),
            dma((2, ys)),
            dma((big_y,)),
            dma((big_y,)),
            dma((ys, big_x)),
            dma((ys, big_x)),
            dma((xs,)),
            dma((xs,)),
            dma((zs,)),
            dma((zs,)),
        ],
        compiler_params=pltpu.CompilerParams(
            collective_id=1, has_side_effects=True, vmem_limit_bytes=60 * 1024 * 1024
        ),
    )(
        feature_table,
        hubs,
        first_self,
        first_pooled,
        second_self,
        second_pooled,
        packed,
        first_counts[:, None],
    )


def solution(mesh):
    return jax.shard_map(
        body,
        mesh=mesh,
        in_specs=(
            P("node", "feat"),
            P("node", "feat"),
            P("feat", None),
            P("feat", None),
            P("feat", None),
            P("feat", None),
            P("node", None),
            P("node"),
            P("node", None),
            P("node"),
        ),
        out_specs=P(("node", "feat"), None),
        check_vma=False,
    )
```

```python
import functools

import jax
import jax.numpy as jnp
from jax import lax
from jax.experimental import pallas as pl
from jax.experimental.pallas import tpu as pltpu
from jax.sharding import PartitionSpec as P

MESH = pl.DeviceIdType.MESH
CORES = 2


def greet(peers):
    barrier = pltpu.get_barrier_semaphore()
    for peer in peers:
        pl.semaphore_signal(barrier, inc=1, device_id=peer, device_id_type=MESH)
    pl.semaphore_wait(barrier, len(peers))


def remote(src, dst, sends, recvs, peer):
    return pltpu.make_async_remote_copy(
        src_ref=src, dst_ref=dst, send_sem=sends, recv_sem=recvs, device_id=peer, device_id_type=MESH
    )


def count_tiles(local, fan, width, store):
    rows = local.shape[0]
    local = local.astype(jnp.int16)
    one, zero = jnp.bfloat16(1), jnp.bfloat16(0)
    for start in range(0, width, 128):
        columns = (lax.broadcasted_iota(jnp.int32, (rows, 128), 1) + start).astype(jnp.int16)
        total = jnp.zeros((rows, 128), jnp.bfloat16)
        for k in range(fan):
            picked = jnp.broadcast_to(local[:, k : k + 1], (rows, 128))
            total = total + jnp.where(picked == columns, one, zero)
        store(start, total)


def main_kernel(
    sizes,
    table_ref,
    hub_ref,
    self_one,
    pool_one,
    self_two,
    pool_two,
    packed_ref,
    counts_ref,
    out_ref,
    lists,
    local,
    tables,
    matrix,
    matrix_two,
    weights,
    means,
    acc,
    z_send,
    z_recv,
    part,
    c_send,
    c_recv,
    y_send,
    y_recv,
    own_ref,
    mixed,
    mc_send,
    mc_recv,
    my_send,
    my_recv,
    mx_send,
    mx_recv,
    acc_z,
    mz_send,
    mz_recv,
    n_ss,
    n_rs,
    x_ss,
    x_rs,
    h_ss,
    h_rs,
    z_ss,
    z_rs,
    c_ss,
    c_rs,
    y_ss,
    y_rs,
    mc_ss,
    mc_rs,
    my_ss,
    my_rs,
    mx_ss,
    mx_rs,
    mz_ss,
    mz_rs,
):
    big_z, big_x, big_y, fan_one, fan_two, hubs_here, edges = sizes
    f32, bf16 = jnp.float32, jnp.bfloat16
    node = lax.axis_index("node")
    feat = lax.axis_index("feat")
    z, x = node // big_x, lax.rem(node, big_x)
    y, core = feat // CORES, lax.rem(feat, CORES)
    x_peers = [{"node": z * big_x + lax.rem(x + o, big_x)} for o in range(1, big_x)]
    z_peers = [{"node": lax.rem(z + o, big_z) * big_x + x} for o in range(1, big_z)]
    y_peers = [{"feat": lax.rem(y + o, big_y) * CORES + core} for o in range(1, big_y)]
    other = 1 - core
    c_peer = {"feat": y * CORES + other}
    shards = big_z * big_x
    n_peers = [{"node": lax.rem(node + o, shards)} for o in range(1, shards)]
    greet(n_peers + y_peers + [c_peer])

    rows, width = table_ref.shape
    front = acc.shape[0]
    reach = tables.shape[1]
    halves = len(edges) - 1

    list_copies = []
    for o, peer in enumerate(n_peers):
        copy = remote(packed_ref, lists.at[node], n_ss.at[o], n_rs.at[o], peer)
        copy.start()
        list_copies.append(copy)
    table_copies = []
    for h in range(halves):
        cut = pl.ds(edges[h], edges[h + 1] - edges[h])
        for o, peer in enumerate(x_peers):
            copy = remote(
                table_ref.at[:, cut],
                tables.at[1 + o, pl.ds(0, rows), cut],
                x_ss.at[h, o],
                x_rs.at[h, o],
                peer,
            )
            copy.start()
            table_copies.append(copy)
        if h == 0:
            for o, peer in enumerate(x_peers):
                copy = remote(
                    hub_ref,
                    tables.at[1 + o, pl.ds(rows, hub_ref.shape[0])],
                    h_ss.at[o],
                    h_rs.at[o],
                    peer,
                )
                copy.start()
                table_copies.append(copy)
    first_copies = 2 * len(x_peers)
    lists[node] = packed_ref[...]
    tail = rows + hub_ref.shape[0]
    tables[0, 0:rows] = table_ref[...]
    tables[0, rows:tail] = hub_ref[...]
    for slot in range(big_x):
        tables[slot, tail:reach] = jnp.zeros((reach - tail, width), bf16)
    for copy in list_copies:
        copy.wait()

    def decode(n, carry):
        entry = lists[n]
        found = jnp.full(entry.shape, -1, jnp.int32)
        for slot in range(big_x):
            owner = z * big_x + lax.rem(x - slot + big_x, big_x)
            feature_at = entry - owner * rows
            hub_at = entry - shards * rows - owner * hubs_here
            found = jnp.where(
                (feature_at >= 0) & (feature_at < rows), feature_at + slot * reach, found
            )
            found = jnp.where(
                (hub_at >= 0) & (hub_at < hubs_here), hub_at + (slot * reach + rows), found
            )
        line = lax.broadcasted_iota(jnp.int32, entry.shape, 0)
        seconds = jnp.clip(entry - node * front, -1, front)
        seconds = jnp.where(line == fan_one + fan_two, entry, seconds)
        local[n] = jnp.where(line < fan_one, found, seconds).T
        return carry

    lax.fori_loop(0, shards, decode, 0)

    def fill(target, at):
        def step(i, carry):
            row0 = pl.multiple_of(i * 32, 32)

            def store(start, value):
                matrix[at, pl.ds(row0, 32), start : start + 128] = value

            count_tiles(local[target, pl.ds(row0, 32), :], fan_one, reach * big_x, store)
            return carry

        lax.fori_loop(0, front // 32, step, 0)

    def sums_of(at, top, deep, low, high):
        total = jnp.dot(matrix[at, top : top + deep, 0:reach], tables[0, :, low:high], preferred_element_type=f32)
        for slot in range(1, big_x):
            total = total + jnp.dot(
                matrix[at, top : top + deep, slot * reach : (slot + 1) * reach],
                tables[slot, :, low:high],
                preferred_element_type=f32,
            )
        return total

    half = front // 2
    pieces = [(h, 0, front, edges[h], edges[h + 1]) for h in range(halves)]
    if halves > 1:
        last = pieces.pop()
        pieces += [(last[0], r * half, half, last[3], last[4]) for r in range(2)]

    def z_copy(p, s, to):
        peer = {"node": to * big_x + x}
        _, top, deep, low, high = pieces[p]
        at = (s, pl.ds(top, deep), pl.ds(low, high - low))
        return remote(z_send.at[at], z_recv.at[at], z_ss.at[p, s], z_rs.at[p, s], peer)

    slots = matrix.shape[0]
    fill(lax.rem(z + 1, big_z) * big_x + x, 0)
    for copy in table_copies[:first_copies]:
        copy.wait()

    def first_half(s, carry):
        zt = lax.rem(z + 1 + s, big_z)
        at = lax.rem(s, slots)

        @pl.when(s > 0)
        def _():
            fill(zt * big_x + x, at)

        z_send[s, :, 0 : edges[1]] = sums_of(at, 0, front, 0, edges[1]).astype(bf16)
        z_copy(0, s, zt).start()
        return carry

    lax.fori_loop(0, big_z - 1, first_half, 0)
    for p in range(1, len(pieces)):
        h, top, deep, low, high = pieces[p]
        if top == 0:
            begin = first_copies + (h - 1) * len(x_peers)
            for copy in table_copies[begin : begin + len(x_peers)]:
                copy.wait()

        def other_piece(s, carry, p=p, top=top, deep=deep, low=low, high=high):
            z_send[s, top : top + deep, low:high] = sums_of(s, top, deep, low, high).astype(bf16)
            z_copy(p, s, lax.rem(z + 1 + s, big_z)).start()
            return carry

        lax.fori_loop(0, big_z - 1, other_piece, 0)
    fill(node, 0)
    acc[...] = sums_of(0, 0, front, 0, width)

    hidden_part = part.shape[2]
    feats = big_y * CORES

    def own_part(f, carry):
        at = pl.ds(pl.multiple_of(f * hidden_part, 128), hidden_part)
        part[f] = jnp.dot(table_ref[0:front, :], self_one[:, at], preferred_element_type=f32)
        return carry

    lax.fori_loop(0, feats, own_part, 0)

    piece = out_ref.shape[0]

    def fill_two(at, carry):
        n, f = at // feats, lax.rem(at, feats)
        zz, xx = n // big_x, lax.rem(n, big_x)
        yy, cc = f // CORES, lax.rem(f, CORES)
        to = (((cc * big_y + yy) * big_x + xx) * big_z + zz) * piece
        from_row = pl.multiple_of(f * piece, 16)
        to_row = pl.multiple_of(to, 16)
        block = local[n, pl.ds(from_row, piece), :]

        def store(start, value):
            matrix_two[pl.ds(to_row, piece), start : start + 128] = value

        count_tiles(block[:, fan_one : fan_one + fan_two], fan_two, front, store)
        weights[pl.ds(to_row, piece), :] = 1.0 / block[
            :, fan_one + fan_two : fan_one + fan_two + 1
        ].astype(f32)
        return carry

    lax.fori_loop(0, shards * feats, fill_two, 0)

    def c_copy(r, s):
        at = (s, pl.ds(r * half, half))
        return remote(c_send.at[at], c_recv.at[at], c_ss.at[r, s], c_rs.at[r, s], c_peer)

    def y_copy(r, s, to):
        peer = {"feat": to * CORES + core}
        at = (s, pl.ds(r * half, half))
        return remote(y_send.at[at], y_recv.at[at], y_ss.at[r, s], y_rs.at[r, s], peer)

    for r in range(2):
        top, end = r * half, (r + 1) * half
        for p, (_, first, deep, low, high) in enumerate(pieces):
            if first == top:
                for s in range(big_z - 1):
                    z_copy(p, s, lax.rem(z + 1 + s, big_z)).wait()
                    acc[first : first + deep, low:high] += z_recv[
                        s, first : first + deep, low:high
                    ].astype(f32)
        means[top:end, :] = (acc[top:end, :] / counts_ref[top:end, :].astype(f32)).astype(bf16)

        def part_of(f, top=top, end=end):
            at = pl.ds(pl.multiple_of(f * hidden_part, 128), hidden_part)
            return part[f, top:end, :] + jnp.dot(
                means[top:end, :], pool_one[:, at], preferred_element_type=f32
            )

        def c_phase(s, carry, r=r, top=top, end=end, part_of=part_of):
            yt = lax.rem(y + 1 + s, big_y)
            c_send[s, top:end, :] = part_of(yt * CORES + other).astype(bf16)
            c_copy(r, s).start()
            return carry

        lax.fori_loop(0, big_y, c_phase, 0)

        def y_step(s, carry, r=r, top=top, end=end, part_of=part_of):
            yt = lax.rem(y + 1 + s, big_y)
            total = part_of(yt * CORES + core)
            c_copy(r, s).wait()
            total = total + c_recv[s, top:end, :].astype(f32)

            @pl.when(s < big_y - 1)
            def _():
                y_send[s, top:end, :] = total.astype(bf16)
                y_copy(r, s, yt).start()

            @pl.when(s == big_y - 1)
            def _():
                part[0, top:end, :] = total

            return carry

        lax.fori_loop(0, big_y, y_step, 0)
    total = part[0]
    for s in range(big_y - 1):
        for r in range(2):
            y_copy(r, s, lax.rem(y + 1 + s, big_y)).wait()
        total = total + y_recv[s].astype(f32)
    hidden = jnp.maximum(total, 0.0).astype(bf16)

    projected = jnp.dot(hidden, pool_two[...], preferred_element_type=f32).astype(bf16)
    own_ref[...] = jnp.dot(hidden[0 : piece * feats], self_two[...], preferred_element_type=f32)
    quarter = big_x * big_z * piece
    slab = big_z * piece

    def mix(k, s, c, yy):
        at = pl.ds(pl.multiple_of((c * big_y + yy) * quarter, 16), quarter)
        mixed[k, s] = (
            jnp.dot(matrix_two[at, :], projected, preferred_element_type=f32) * weights[at, :]
        )
        row = pl.multiple_of((x * big_z + z) * piece, 16)
        from_row = pl.multiple_of((yy * CORES + c) * piece, 16)
        mixed[k, s, pl.ds(row, piece), :] += own_ref[pl.ds(from_row, piece), :]

    core_copies = []
    for s in range(big_y):
        mix(0, s, other, lax.rem(y + 1 + s, big_y))
        mc_send[s] = mixed[0, s].astype(bf16)
        copy = remote(mc_send.at[s], mc_recv.at[s], mc_ss.at[s], mc_rs.at[s], c_peer)
        copy.start()
        core_copies.append(copy)
    for s in range(big_y):
        mix(1, s, core, lax.rem(y + 1 + s, big_y))
    x_rows = [
        pl.ds(pl.multiple_of(lax.rem(x + 1 + o, big_x) * slab, 16), slab) for o in range(big_x)
    ]
    y_copies = {}
    for s in range(big_y):
        core_copies[s].wait()
        mixed[1, s] += mc_recv[s].astype(f32)
        if s < big_y - 1:
            for o in range(big_x):
                my_send[s, o] = mixed[1, s, x_rows[o], :].astype(bf16)
                copy = remote(
                    my_send.at[s, o], my_recv.at[s, o], my_ss.at[s, o], my_rs.at[s, o], y_peers[s]
                )
                copy.start()
                y_copies[s, o] = copy
    x_copies = []
    for o in range(big_x):
        total = mixed[1, big_y - 1, x_rows[o], :]
        for s in range(big_y - 1):
            y_copies[s, o].wait()
            total = total + my_recv[s, o].astype(f32)
        if o < big_x - 1:
            mx_send[o] = total.astype(bf16)
            copy = remote(mx_send.at[o], mx_recv.at[o], mx_ss.at[o], mx_rs.at[o], x_peers[o])
            copy.start()
            x_copies.append(copy)
    for o, copy in enumerate(x_copies):
        copy.wait()
        total = total + mx_recv[o].astype(f32)
    acc_z[...] = total
    mz_send[...] = total.astype(bf16)
    z_copies = []
    for o in range(big_z - 1):
        row = pl.multiple_of(lax.rem(z + 1 + o, big_z) * piece, 16)
        copy = remote(
            mz_send.at[pl.ds(row, piece)], mz_recv.at[o], mz_ss.at[o], mz_rs.at[o], z_peers[o]
        )
        copy.start()
        z_copies.append(copy)
    total = acc_z[pl.ds(pl.multiple_of(z * piece, 8), piece), :]
    for o, copy in enumerate(z_copies):
        copy.wait()
        total = total + mz_recv[o].astype(f32)
    scale = lax.rsqrt(jnp.mean(total * total, axis=1, keepdims=True) + 1e-06)
    out_ref[...] = (total * scale).astype(bf16)


def body(
    feature_table,
    hub_table,
    first_self,
    first_pooled,
    second_self,
    second_pooled,
    first_lists,
    first_counts,
    second_lists,
    second_counts,
):
    shards = lax.axis_size("node")
    feats = lax.axis_size("feat")
    big_x = 2 ** ((shards.bit_length() - 1) // 2)
    big_z = shards // big_x
    big_y = feats // CORES
    rows_here, width = feature_table.shape
    hubs_here = hub_table.shape[0]
    front, fan_one = first_lists.shape
    targets_here, fan_two = second_lists.shape
    piece = targets_here // feats
    out_width = second_self.shape[1]
    hidden_part = second_self.shape[0]

    slots_one = jnp.arange(fan_one, dtype=jnp.int32)[None, :]
    slots_two = jnp.arange(fan_two, dtype=jnp.int32)[None, :]
    lists_one = jnp.where(slots_one < first_counts[:, None], first_lists, -1).T
    lists_two = jnp.where(slots_two < second_counts[:, None], second_lists, -1).T
    lists_two = jnp.concatenate([lists_two, second_counts[None, :]], axis=0)
    lists_two = jnp.pad(lists_two, ((0, 0), (0, front - targets_here)))
    packed = jnp.concatenate([lists_one, lists_two], axis=0)
    hubs = jnp.pad(hub_table, ((0, -hubs_here % 16), (0, 0)))
    reach = rows_here + 128
    edges = (0, 128, 256, width) if width > 256 else (0, width)
    chunks = len(edges) if len(edges) > 2 else 1
    bf16, f32 = jnp.bfloat16, jnp.float32
    dma = pltpu.SemaphoreType.DMA
    zs, xs, ys = big_z - 1, big_x - 1, big_y - 1
    quarter = big_x * big_z * piece
    slab = big_z * piece
    block = (front, width)
    hblock = (front, hidden_part)
    vmem = pl.BlockSpec(memory_space=pltpu.VMEM)
    return pl.pallas_call(
        functools.partial(main_kernel, (big_z, big_x, big_y, fan_one, fan_two, hubs_here, edges)),
        out_shape=jax.ShapeDtypeStruct((piece, out_width), bf16),
        in_specs=[vmem] * 8,
        out_specs=vmem,
        scratch_shapes=[
            pltpu.VMEM((shards,) + packed.shape, jnp.int32),
            pltpu.VMEM((shards, front, packed.shape[0]), jnp.int32),
            pltpu.VMEM((big_x, reach, width), bf16),
            pltpu.VMEM((zs if chunks > 1 else 1, front, big_x * reach), bf16),
            pltpu.VMEM((targets_here * shards, front), bf16),
            pltpu.VMEM((targets_here * shards, 1), f32),
            pltpu.VMEM(block, bf16),
            pltpu.VMEM(block, f32),
            pltpu.VMEM((zs,) + block, bf16),
            pltpu.VMEM((zs,) + block, bf16),
            pltpu.VMEM((feats,) + hblock, f32),
            pltpu.VMEM((big_y,) + hblock, bf16),
            pltpu.VMEM((big_y,) + hblock, bf16),
            pltpu.VMEM((ys,) + hblock, bf16),
            pltpu.VMEM((ys,) + hblock, bf16),
            pltpu.VMEM((targets_here, out_width), f32),
            pltpu.VMEM((CORES, big_y, quarter, out_width), f32),
            pltpu.VMEM((big_y, quarter, out_width), bf16),
            pltpu.VMEM((big_y, quarter, out_width), bf16),
            pltpu.VMEM((ys, big_x, slab, out_width), bf16),
            pltpu.VMEM((ys, big_x, slab, out_width), bf16),
            pltpu.VMEM((xs, slab, out_width), bf16),
            pltpu.VMEM((xs, slab, out_width), bf16),
            pltpu.VMEM((slab, out_width), f32),
            pltpu.VMEM((slab, out_width), bf16),
            pltpu.VMEM((zs, piece, out_width), bf16),
            dma((shards - 1,)),
            dma((shards - 1,)),
            dma((len(edges) - 1, xs)),
            dma((len(edges) - 1, xs)),
            dma((xs,)),
            dma((xs,)),
            dma((chunks, zs)),
            dma((chunks, zs)),
            dma((2, big_y)),
            dma((2, big_y)),
            dma((2, ys)),
            dma((2, ys)),
            dma((big_y,)),
            dma((big_y,)),
            dma((ys, big_x)),
            dma((ys, big_x)),
            dma((xs,)),
            dma((xs,)),
            dma((zs,)),
            dma((zs,)),
        ],
        compiler_params=pltpu.CompilerParams(
            collective_id=1, has_side_effects=True, vmem_limit_bytes=60 * 1024 * 1024
        ),
    )(
        feature_table,
        hubs,
        first_self,
        first_pooled,
        second_self,
        second_pooled,
        packed,
        first_counts[:, None],
    )


def solution(mesh):
    return jax.shard_map(
        body,
        mesh=mesh,
        in_specs=(
            P("node", "feat"),
            P("node", "feat"),
            P("feat", None),
            P("feat", None),
            P("feat", None),
            P("feat", None),
            P("node", None),
            P("node"),
            P("node", None),
            P("node"),
        ),
        out_specs=P(("node", "feat"), None),
        check_vma=False,
    )
```
